32 devices in a mesh: group: 16 (over z, x, core), dom: 2 (over y).
Axes of the slice: x: 2, y: 2, z: 4, core: 2. Of those that a mesh axis runs over, the one named last changes fastest.
Arguments:
- state: float32 [4, 16, 15600], P(None, 'group', 'dom'), may hold values from -6 to 6
- mesh_vel: float32 [3, 16, 15600], P(None, 'group', 'dom'), may hold values from -6 to 6
- disp: float32 [3, 16, 15600], P(None, 'group', 'dom'), may hold values from -6 to 6
- elem_size: float32 [16, 8192], P('group', 'dom'), may hold values from 0.5 to 2
- live_slabs: int32 [16, 2], P('group', 'dom'), may hold values from 1 to 4
- trace_rows: int32 [16, 2, 4, 1024], P('group', 'dom'), may hold values from 0 to 7799, as said below
- penalty: float32 [16, 2, 4, 1024], P('group', 'dom'), may hold values from 1 to 4
Outputs:
- residual: float32 [4, 16, 15600], P(None, 'group', 'dom')
- new_disp: float32 [3, 16, 15600], P(None, 'group', 'dom')
The draws below stay inside these ranges and needn't reach their ends.
Inputs may be any that keep to these rules, and one draw needn't show every extreme that they name: `trace_rows`: rows of the element block itself, on its faces where the second index is 0 or 9 or the third index is 0 or 129.
All inputs are finite; a program needn't handle non-finite values.
Results may differ from the reference program's by a relative error of at most 0.0003.
Values sent between devices are 32-bit elements; how exact they have to be, the bound alone decides.
A program may use at most 64 MiB of HBM per device.

```python
import math
import jax
import jax.numpy as jnp
from jax import lax

PA = 6
PB = 10
PC = 130
SLOTS = 1024
CP = 7800
SLABS = 4
EPS = 1024
ELEMS = 4096
N_GROUP = 16
N_DOM = 2


def draw_live_slabs(key, part):
    drawn = jax.random.randint(key, (N_GROUP, N_DOM), 1, SLABS + 1)
    drawn = drawn.at[0, 0].set(SLABS)
    drawn = drawn.at[N_GROUP - 1, N_DOM - 1].set(1)
    return drawn.astype(jnp.int32)


def draw_trace_rows(key, part):
    key_face, key_plane, key_b, key_c = jax.random.split(jax.random.fold_in(key, 11), 4)
    shape = (N_GROUP, N_DOM, 4, SLOTS)
    face = jax.random.randint(key_face, shape, 0, 4)
    plane = jax.random.randint(key_plane, shape, 0, PA)
    along_b = jax.random.randint(key_b, shape, 0, PB)
    along_c = jax.random.randint(key_c, shape, 0, PC)
    index_b = jnp.where(face == 0, 0, jnp.where(face == 1, PB - 1, along_b))
    index_c = jnp.where(face == 2, 0, jnp.where(face == 3, PC - 1, along_c))
    rows = (plane * PB + index_b) * PC + index_c
    rows = rows.at[0, 0, 0, 0].set(0)
    rows = rows.at[0, 0, 0, 1].set(CP - 1)
    return rows.astype(jnp.int32)


def block_levels(stream_key, dims, shards, least, largest):
    factor_of = 1.0
    for dim, shards_of in shards:
        draws = jax.random.uniform(jax.random.fold_in(jax.random.fold_in(stream_key, 6), dim), (shards_of,), jnp.float32, least / len(shards), largest / len(shards))
        factor_of = factor_of * jnp.repeat(jnp.exp(draws), dims[dim] // shards_of).reshape((-1,) + (1,) * (len(dims) - 1 - dim))
    return factor_of


def noise(own_key, extent, width, reach, cuts=(), kind=jnp.bfloat16):
    values = width * jax.random.normal(own_key, extent, jnp.float32)
    if cuts:
        values = values * block_levels(own_key, extent, cuts, -0.22, 0.18)
    return jnp.clip(values, -reach, reach).astype(kind)


def setup_inputs(seed: int = 0) -> dict:
    seeds = jax.random.split(jax.random.key(seed), 8)
    state = noise(seeds[0], (4, N_GROUP, N_DOM * CP), 1.0, 6.0, ((1, 16), (2, 2)), jnp.float32)
    mesh_vel = noise(seeds[1], (3, N_GROUP, N_DOM * CP), 1.0, 6.0, ((1, 16), (2, 2)), jnp.float32)
    disp = noise(seeds[2], (3, N_GROUP, N_DOM * CP), 1.0, 6.0, ((1, 16), (2, 2)), jnp.float32)
    elem_size = jnp.clip(jnp.exp(math.log(2.0) - 1.3862944 * jax.random.uniform(seeds[3], (N_GROUP, N_DOM * ELEMS), jnp.float32) ** block_levels(seeds[3], (N_GROUP, N_DOM * ELEMS), ((0, 16), (1, 2)), -0.2, 0.2)), 0.5, 2.0)
    live_slabs = draw_live_slabs(jax.random.fold_in(seeds[7], 71), 0)
    trace_rows = draw_trace_rows(jax.random.fold_in(seeds[7], 71), 0)
    penalty = jnp.clip(jnp.exp(math.log(4.0) - 1.3862944 * jax.random.uniform(seeds[6], (N_GROUP, N_DOM, 4, SLOTS), jnp.float32) ** block_levels(seeds[6], (N_GROUP, N_DOM, 4, SLOTS), ((0, 16), (1, 2)), -0.2, 0.2)), 1.0, 4.0)
    return dict(state=state, mesh_vel=mesh_vel, disp=disp, elem_size=elem_size, live_slabs=live_slabs, trace_rows=trace_rows, penalty=penalty)


time_step = 0.5
viscosity = 0.05

def basis_tables():
    points = jnp.array([0.5 - math.sqrt(0.15), 0.5, 0.5 + math.sqrt(0.15)], jnp.float32)
    gauss_weights = jnp.array([5.0 / 18.0, 8.0 / 18.0, 5.0 / 18.0], jnp.float32)
    column = points[:, None]
    values = jnp.concatenate([(1.0 - column) ** 2 / 2.0, (1.0 + 2.0 * column - 2.0 * column ** 2) / 2.0, column ** 2 / 2.0], axis=1)
    slopes = jnp.concatenate([column - 1.0, 1.0 - 2.0 * column, column], axis=1)

    def triple(along_a, along_b, along_c):
        return jnp.einsum('ia,jb,kc->ijkabc', along_a, along_b, along_c).reshape(27, 27)
    stacked = jnp.concatenate([triple(values, values, values), triple(slopes, values, values), triple(values, slopes, values), triple(values, values, slopes)], axis=0)
    quad_weights = jnp.einsum('i,j,k->ijk', gauss_weights, gauss_weights, gauss_weights).reshape(27)
    return (stacked, quad_weights)

def element_terms(planes, mesh_planes, sizes):
    stacked, quad_weights = basis_tables()
    inner_b = PB - 2
    inner_c = PC - 2

    def gather_local(cp_block):
        return jnp.stack([cp_block[:, shift_a, shift_b:shift_b + inner_b, shift_c:shift_c + inner_c].reshape(cp_block.shape[0], EPS) for shift_a in range(3) for shift_b in range(3) for shift_c in range(3)], axis=0)
    local_vals = gather_local(planes)
    local_mesh = gather_local(mesh_planes)
    at_points = jnp.dot(stacked, local_vals.reshape(27, 4 * EPS), precision=lax.Precision.HIGHEST, preferred_element_type=jnp.float32).reshape(4, 27, 4, EPS)
    mesh_points = jnp.dot(stacked[:27], local_mesh.reshape(27, 3 * EPS), precision=lax.Precision.HIGHEST, preferred_element_type=jnp.float32).reshape(27, 3, EPS)
    values_q = at_points[0]
    slopes_q = [at_points[1 + direction] / sizes for direction in range(3)]
    advect = values_q[:, :3] - mesh_points
    convect = advect[:, 0:1] * slopes_q[0][:, :3] + advect[:, 1:2] * slopes_q[1][:, :3] + advect[:, 2:3] * slopes_q[2][:, :3]
    momentum = convect + jnp.stack([slopes_q[component][:, 3] for component in range(3)], axis=1)
    continuity = slopes_q[0][:, 0] + slopes_q[1][:, 1] + slopes_q[2][:, 2]
    speed_sq = lax.optimization_barrier(jnp.sum(advect * advect, axis=1))
    tau_moment = 1.0 / jnp.sqrt(4.0 / time_step ** 2 + 4.0 * speed_sq / sizes ** 2 + 36.0 * viscosity ** 2 / sizes ** 4)
    tau_contin = sizes ** 2 / (12.0 * tau_moment)
    pressure_part = values_q[:, 3] - tau_contin * continuity
    weight = quad_weights[:, None, None] * (sizes ** 3)[None, None, :]
    pieces = [weight * jnp.concatenate([convect, continuity[:, None]], axis=1)]
    for direction in range(3):
        unit_vector = (jnp.arange(3) == direction).astype(jnp.float32)
        velocity_part = viscosity * slopes_q[direction][:, :3] + (advect[:, direction] * tau_moment)[:, None, :] * momentum - unit_vector[None, :, None] * pressure_part[:, None, :]
        grad_coef = jnp.concatenate([velocity_part, (tau_moment * momentum[:, direction])[:, None, :]], axis=1)
        pieces.append(weight * grad_coef / sizes)
    coefs = jnp.concatenate(pieces, axis=0)
    element_res = jnp.dot(stacked.T, coefs.reshape(108, 4 * EPS), precision=lax.Precision.HIGHEST, preferred_element_type=jnp.float32).reshape(27, 4, EPS)
    contrib = jnp.zeros((4, 3, PB, PC), jnp.float32)
    position = 0
    for shift_a in range(3):
        for shift_b in range(3):
            for shift_c in range(3):
                contrib = contrib.at[:, shift_a, shift_b:shift_b + inner_b, shift_c:shift_c + inner_c].add(element_res[position].reshape(4, inner_b, inner_c))
                position += 1
    return contrib

def block_residual(values, mesh_field, sizes, live_count):
    cp_grid = values.reshape(4, PA, PB, PC)
    mesh_grid = mesh_field.reshape(3, PA, PB, PC)

    def slab(slab_index, summed):
        planes = lax.dynamic_slice_in_dim(cp_grid, slab_index, 3, 1)
        mesh_planes = lax.dynamic_slice_in_dim(mesh_grid, slab_index, 3, 1)
        slab_sizes = lax.dynamic_slice_in_dim(sizes, slab_index * EPS, EPS)
        contrib = element_terms(planes, mesh_planes, slab_sizes) * (slab_index < live_count).astype(jnp.float32)
        current = lax.dynamic_slice_in_dim(summed, slab_index, 3, 1)
        return lax.dynamic_update_slice_in_dim(summed, current + contrib, slab_index, 1)
    summed = lax.fori_loop(0, SLABS, slab, jnp.zeros((4, PA, PB, PC), jnp.float32))
    return summed.reshape(4, CP)

def reference(state, mesh_vel, disp, elem_size, live_slabs, trace_rows, penalty):
    groups = N_GROUP
    doms = N_DOM
    blocks = groups * doms
    by_block = state.reshape(4, blocks, CP).transpose(1, 0, 2)
    mesh_block = mesh_vel.reshape(3, blocks, CP).transpose(1, 0, 2)
    disp_block = disp.reshape(3, blocks, CP).transpose(1, 0, 2)
    sizes = elem_size.reshape(blocks, ELEMS)
    counts_live = live_slabs.reshape(blocks)
    local = lax.map(lambda item: block_residual(item[0], item[1], item[2], item[3]), (by_block, mesh_block, sizes, counts_live))
    local = local.reshape(groups, doms, 4, PA, PB * PC)
    assembled = local.at[:, 1:, :, :2].add(local[:, :-1, :, -2:])
    assembled = assembled.at[:, :-1, :, -2:].add(local[:, 1:, :, :2])
    moved = (disp_block + 0.5 * mesh_block).reshape(groups, doms, 3, PA, PB * PC)
    shared_shift = jnp.zeros_like(moved)
    shared_shift = shared_shift.at[:, 1:, :, :2].add(0.5 * (moved[:, :-1, :, -2:] - moved[:, 1:, :, :2]))
    shared_shift = shared_shift.at[:, :-1, :, -2:].add(0.5 * (moved[:, 1:, :, :2] - moved[:, :-1, :, -2:]))
    assembled = assembled.reshape(groups, doms, 4, CP)
    moved = moved.reshape(groups, doms, 3, CP)
    shared_shift = shared_shift.reshape(groups, doms, 3, CP)
    values = by_block.reshape(groups, doms, 4, CP)
    rows = trace_rows.astype(jnp.int32)
    stride = groups // 2
    offsets = jnp.array([1, -1, stride, -stride], jnp.int32)
    own_g = jnp.arange(groups, dtype=jnp.int32)[:, None, None, None]
    own_d = jnp.arange(doms, dtype=jnp.int32)[None, :, None, None]
    which = jnp.arange(4, dtype=jnp.int32)
    flip = jnp.array([1, 0, 3, 2], jnp.int32)[None, None, :, None]
    slot_idx = jnp.arange(SLOTS, dtype=jnp.int32)[None, None, None, :]
    peer_raw = own_g + offsets[which][None, None, :, None]
    present = (peer_raw >= 0) & (peer_raw < groups)
    peer_g = jnp.clip(peer_raw, 0, groups - 1).astype(jnp.int32)
    partner = rows[peer_g, own_d, flip, slot_idx]
    valid = present.astype(jnp.float32)
    gammas = penalty[..., None]
    mask = valid[..., None]
    term = mask * (gammas * (values[own_g, own_d, :, rows] - values[peer_g, own_d, :, partner]) + 0.5 * (assembled[peer_g, own_d, :, partner] - assembled[own_g, own_d, :, rows]))
    residual = assembled.at[own_g, own_d, :, rows].add(term)
    counted = jnp.zeros((groups, doms, CP), jnp.int32).at[own_g, own_d, rows].add(jnp.broadcast_to(present, rows.shape).astype(jnp.int32))
    differ = mask * (moved[peer_g, own_d, :, partner] - moved[own_g, own_d, :, rows])
    disp_sum = jnp.zeros((groups, doms, 3, CP), jnp.float32).at[own_g, own_d, :, rows].add(differ)
    divisor = 2.0 * jnp.maximum(counted, 1).astype(jnp.float32)
    new_disp = moved + shared_shift + disp_sum / divisor[:, :, None, :]
    residual = residual.transpose(2, 0, 1, 3).reshape(4, groups, doms * CP)
    new_disp = new_disp.transpose(2, 0, 1, 3).reshape(3, groups, doms * CP)
    return (residual, new_disp)
```

```python
import functools
import math

import jax
import jax.numpy as jnp
from jax import lax
from jax.experimental import pallas as pl
from jax.experimental.pallas import tpu as pltpu
from jax.sharding import PartitionSpec as P

PA = 6
PB = 10
PC = 130
CP = PA * PB * PC
SLABS = 4
ROWS = PA * PB
PLANE = PB * PC
LANES = 128
COLS = 61
WIDE = (COLS + 1) * LANES
SLOTS = 1024
SHARED = 2 * PLANE
RIM = 21 * LANES
LAST_COL = 4 * PLANE // LANES
LAST_OFF = 4 * PLANE % LANES
TABS = 14

DT = 0.5
NU = 0.05
S = math.sqrt(0.15)
W_EDGE = 5.0 / 18.0
W_MID = 8.0 / 18.0
F32 = jnp.float32
BF16 = jnp.bfloat16


def face_extras():
    out = []
    for a in range(PA):
        base = a * PLANE
        out += [base + b * PC + 129 for b in range(PB)]
        out += [base + 128, base + 9 * PC + 128]
        out += [base + b * PC for b in range(1, PB - 1)]
    return out


EXTRAS = face_extras()


def lane_iota():
    return lax.broadcasted_iota(jnp.int32, (8, LANES), 1)


def take_row(ref, start):
    off = start % LANES
    col = start - off
    first = ref[:, col : col + LANES]
    if off == 0:
        return first
    second = ref[:, col + LANES : col + 2 * LANES]
    mixed = jnp.where(lane_iota() >= off, first, second)
    return pltpu.roll(mixed, LANES - off, 1)


def add_row(ref, start, val):
    off = start % LANES
    col = start - off
    if off == 0:
        ref[:, col : col + LANES] += val
        return
    turned = pltpu.roll(val, off, 1)
    lane = lane_iota()
    ref[:, col : col + LANES] += jnp.where(lane >= off, turned, 0.0)
    ref[:, col + LANES : col + 2 * LANES] += jnp.where(lane < off, turned, 0.0)


def locate(row):
    plane = jnp.zeros_like(row)
    for k in range(1, PA):
        plane = plane + (row >= k * PLANE).astype(jnp.int32)
    rest = row - plane * PLANE
    along_b = jnp.zeros_like(row)
    for k in range(1, PB):
        along_b = along_b + (rest >= k * PC).astype(jnp.int32)
    along_c = rest - along_b * PC
    top = along_b == PB - 1
    straight = ((along_b == 0) | top) & (along_c < LANES)
    which = jnp.where(
        along_c == 129,
        along_b,
        jnp.where(along_c == 128, jnp.where(top, 11, 10), 11 + along_b),
    )
    hi = jnp.where(straight, 2 * plane + top.astype(jnp.int32), 12)
    lo = jnp.where(straight, along_c, 20 * plane + which)
    return hi, lo


def one_hot(lo):
    return (lax.broadcasted_iota(jnp.int32, (LANES, SLOTS), 0) == lo).astype(F32).astype(BF16)


def split_bf16(val):
    high = val.astype(BF16)
    low = (val - high.astype(F32)).astype(BF16)
    return high, low


def face_tables(x_ref, tab_ref):
    lane = lane_iota()
    for a in range(PA):
        tab_ref[16 * a : 16 * a + 8, :] = take_row(x_ref, a * PLANE)
        tab_ref[16 * a + 8 : 16 * a + 16, :] = take_row(x_ref, a * PLANE + 9 * PC)
    extra = jnp.zeros((8, LANES), F32)
    for k, flat in enumerate(EXTRAS):
        extra = jnp.where(lane == k, x_ref[:, flat : flat + 1], extra)
    tab_ref[96:104, :] = extra
    tab_ref[104:112, :] = jnp.zeros((8, LANES), F32)
    high, low = split_bf16(tab_ref[...])
    return jnp.concatenate([high, low], axis=0)


def gather_slots(table, hi, hot):
    full = jnp.dot(table, hot, preferred_element_type=F32)
    out = jnp.zeros((8, SLOTS), F32)
    for h in range(13):
        piece = full[8 * h : 8 * h + 8] + full[112 + 8 * h : 120 + 8 * h]
        out = jnp.where(hi == h, piece, out)
    return out


def trace_kernel(state_ref, mesh_ref, disp_ref, rows_ref, pay_ref, first_ref, last_ref, x_ref, tab_ref):
    for c in range(3):
        x_ref[c : c + 1, :CP] = disp_ref[c] + 0.5 * mesh_ref[c]
    x_ref[3:4, :CP] = jnp.zeros((1, CP), F32)
    for c in range(4):
        x_ref[4 + c : 5 + c, :CP] = state_ref[c]
    x_ref[:, COLS * LANES :] = jnp.zeros((8, LANES), F32)
    first_ref[...] = x_ref[0:4, :RIM]
    last_ref[...] = x_ref[0:4, LAST_COL * LANES : LAST_COL * LANES + RIM]
    table = face_tables(x_ref, tab_ref)
    for k in range(4):
        hi, lo = locate(rows_ref[k : k + 1, :])
        pay_ref[k] = gather_slots(table, hi, one_hot(lo))


def fwd_value(x0, x1, x2):
    even, odd = x0 + x2, x2 - x0
    base = 0.2 * even + 0.6 * x1
    mid = 0.125 * even + 0.75 * x1
    side = (S / 2) * odd
    return (base - side, mid, base + side)


def fwd_slope(x0, x1, x2):
    half = 0.5 * (x2 - x0)
    bend = S * ((x0 + x2) - 2.0 * x1)
    return (half - bend, half, half + bend)


def back_value(y0, y1, y2):
    even, odd = y0 + y2, y2 - y0
    ends = (W_EDGE * 0.2) * even + (W_MID * 0.125) * y1
    side = (W_EDGE * S / 2) * odd
    return (ends - side, (W_EDGE * 0.6) * even + (W_MID * 0.75) * y1, ends + side)


def back_slope(z0, z1, z2):
    turn = (W_EDGE * S) * (z2 - z0)
    half = (0.5 * W_EDGE) * (z0 + z2) + (0.5 * W_MID) * z1
    return (turn - half, -2.0 * turn, turn + half)


def both(value, slope):
    return tuple(v + d for v, d in zip(back_value(*value), back_slope(*slope)))


def strided(start):
    return pl.ds(start, 8, stride=8)


def element_kernel(
    live_ref, state_ref, mesh_ref, size_ref,
    out_ref, first_ref, last_ref,
    x_ref, q_ref, g_ref, acc_ref, h_ref,
):
    for c in range(4):
        x_ref[c : c + 1, :CP] = state_ref[c]
    for c in range(3):
        x_ref[4 + c : 5 + c, :CP] = state_ref[c] - mesh_ref[c]
    x_ref[7:8, :CP] = jnp.zeros((1, CP), F32)
    for k in range(32):
        h_ref[k // 8, k % 8 : k % 8 + 1, :] = size_ref[:, k * LANES : (k + 1) * LANES]
    for r in range(ROWS):
        taps = [take_row(x_ref, r * PC + s) for s in range(3)]
        for k, val in enumerate(fwd_value(*taps) + fwd_slope(*taps)):
            q_ref[k, 8 * r : 8 * r + 8, :] = val

    def along_b(a, carry):
        for f in range(7):
            for qc in range(3):
                value = [q_ref[qc, strided(a * 80 + 8 * s + f), :] for s in range(3)]
                if f >= 4:
                    for qb, val in enumerate(fwd_value(*value)):
                        g_ref[a, 3 * qb + qc, 8 + f] = val
                    continue
                slope = [q_ref[3 + qc, strided(a * 80 + 8 * s + f), :] for s in range(3)]
                vv = fwd_value(*value)
                dv = fwd_slope(*value)
                vd = fwd_value(*slope)
                for qb in range(3):
                    g_ref[a, 3 * qb + qc, 3 * f] = vv[qb]
                    g_ref[a, 3 * qb + qc, 3 * f + 1] = dv[qb]
                    g_ref[a, 3 * qb + qc, 3 * f + 2] = vd[qb]
        return carry

    lax.fori_loop(0, PA, along_b, 0)

    zero = jnp.zeros((8, LANES), F32)

    def clear(a, carry):
        for q in range(9):
            for k in range(12):
                acc_ref[a, q, k] = zero
        return carry

    lax.fori_loop(0, PA, clear, 0)

    def points(slab, q):
        h = h_ref[slab]

        def taps(slot):
            return [g_ref[slab + s, q, slot] for s in range(3)]

        grads = [
            [fwd_slope(*taps(3 * f)), fwd_value(*taps(3 * f + 1)), fwd_value(*taps(3 * f + 2))]
            for f in range(4)
        ]
        pressure = fwd_value(*taps(9))
        adv = [fwd_value(*taps(12 + c)) for c in range(3)]
        inv = 1.0 / h
        inv2 = inv * inv
        four = 4.0 * inv2
        fixed = 4.0 / DT**2 + (36.0 * NU**2) * (inv2 * inv2)
        h2 = (h * h) * (1.0 / 12.0)
        coef_f = [[None] * 3 for _ in range(4)]
        coef_k = [[[None] * 3 for _ in range(4)] for _ in range(3)]
        for t in range(3):
            a = [adv[c][t] for c in range(3)]
            conv = [
                a[0] * grads[c][0][t] + a[1] * grads[c][1][t] + a[2] * grads[c][2][t]
                for c in range(3)
            ]
            mom = [conv[c] + grads[3][c][t] for c in range(3)]
            cont = grads[0][0][t] + grads[1][1][t] + grads[2][2][t]
            total = fixed + four * (a[0] * a[0] + a[1] * a[1] + a[2] * a[2])
            tau = lax.rsqrt(total)
            press = h * pressure[t] - h2 * (total * tau) * cont
            scaled = [tau * mom[c] for c in range(3)]
            for c in range(3):
                coef_f[c][t] = h * conv[c]
                coef_k[c][3][t] = scaled[c]
                for d in range(3):
                    val = NU * grads[c][d][t] + a[d] * scaled[c]
                    coef_k[d][c][t] = val - press if d == c else val
            coef_f[3][t] = h * cont
        for c in range(4):
            parts = (
                both(coef_f[c], coef_k[0][c]),
                back_value(*coef_k[1][c]),
                back_value(*coef_k[2][c]),
            )
            for k, part in enumerate(parts):
                for s in range(3):
                    acc_ref[slab + s, q, 3 * c + k] += h * part[s]

    def slab_loop(slab, carry):
        def point_loop(q, inner):
            points(slab, q)
            return inner

        return lax.fori_loop(0, 9, point_loop, carry)

    lax.fori_loop(0, live_ref[0, 0], slab_loop, 0)

    def clear_rows(r, carry):
        for k in range(6):
            q_ref[k, pl.ds(pl.multiple_of(r * 8, 8), 8), :] = zero
        return carry

    lax.fori_loop(0, ROWS, clear_rows, 0)

    def back_b(a, carry):
        for c in range(4):
            for qc in range(3):
                pieces = [
                    [acc_ref[a, 3 * qb + qc, 3 * c + k] for qb in range(3)] for k in range(3)
                ]
                straight = both(pieces[0], pieces[1])
                sloped = back_value(*pieces[2])
                for s in range(3):
                    at = strided(a * 80 + 8 * s + 4 + c)
                    q_ref[qc, at, :] += straight[s]
                    q_ref[3 + qc, at, :] += sloped[s]
        return carry

    lax.fori_loop(0, PA, back_b, 0)

    lane = lane_iota()
    pending = zero
    for r in range(ROWS):
        y = [q_ref[k, 8 * r : 8 * r + 8, :] for k in range(6)]
        y0, y1, y2 = both(y[:3], y[3:])
        y1 = pltpu.roll(y1, 1, 1)
        y2 = pltpu.roll(y2, 2, 1)
        main = y0 + jnp.where(lane >= 1, y1, 0.0) + jnp.where(lane >= 2, y2, 0.0)
        tail = jnp.where(lane < 1, y1, 0.0) + jnp.where(lane < 2, y2, 0.0)
        off = 2 * r
        if off:
            main = pltpu.roll(main, off, 1)
            tail = pltpu.roll(tail, off, 1)
        out_ref[:, r * LANES : (r + 1) * LANES] = jnp.where(lane >= off, main, pending)
        pending = jnp.where(lane < off, main, tail)
    out_ref[:, ROWS * LANES : (ROWS + 1) * LANES] = pending
    out_ref[:, COLS * LANES :] = zero
    first_ref[...] = out_ref[4:8, :RIM]
    last_ref[...] = out_ref[4:8, LAST_COL * LANES : LAST_COL * LANES + RIM]


def rim_cut(col):
    return lane_iota() < min(LANES, SHARED - col * LANES)


def widen(rim_ref, wide_ref, low):
    wide_ref[...] = jnp.zeros_like(wide_ref)
    wide_ref[low : low + 4, :RIM] = rim_ref[...]


def assemble_kernel(local_ref, before_ref, after_ref, rows_ref, asm_ref, pay_ref, wide_ref, tab_ref):
    asm_ref[...] = local_ref[...]
    widen(before_ref, wide_ref, 4)
    for col in range(21):
        val = jnp.where(rim_cut(col), take_row(wide_ref, LAST_OFF + col * LANES), 0.0)
        asm_ref[:, col * LANES : (col + 1) * LANES] += val
    widen(after_ref, wide_ref, 4)
    for col in range(21):
        val = jnp.where(rim_cut(col), wide_ref[:, col * LANES : (col + 1) * LANES], 0.0)
        add_row(asm_ref, LAST_COL * LANES + LAST_OFF + col * LANES, val)
    table = face_tables(asm_ref, tab_ref)
    for k in range(4):
        hi, lo = locate(rows_ref[k : k + 1, :])
        pay_ref[k] = gather_slots(table, hi, one_hot(lo))[4:8]


def finish_kernel(
    flag_ref, asm_ref, mesh_ref, disp_ref, rows_ref, pen_ref,
    own_ref, own2_ref, p0_ref, p1_ref, p2_ref, p3_ref, r0_ref, r1_ref, r2_ref, r3_ref,
    before_ref, after_ref,
    res_ref, new_ref,
    x_ref, d_ref, wide_ref, term_ref,
):
    partners = (p0_ref, p1_ref, p2_ref, p3_ref)
    reactions = (r0_ref, r1_ref, r2_ref, r3_ref)
    acc = jnp.zeros((2 * 8 * TABS, LANES), F32)
    for k in range(4):
        live = flag_ref[0, k]
        gap = partners[k][...] - own_ref[k]
        term_ref[...] = gap * live
        term_ref[3:4, :] = jnp.zeros((1, SLOTS), F32) + live
        term_ref[4:8, :] = live * (
            0.5 * (reactions[k][...] - own2_ref[k]) - pen_ref[k : k + 1, :] * gap[4:8]
        )
        term = term_ref[...]
        hi, lo = locate(rows_ref[k : k + 1, :])
        hot = one_hot(lo)
        high = term.astype(BF16).astype(F32)
        low = term - high
        spread = [jnp.where(hi == h, high, 0.0) for h in range(TABS)]
        spread += [jnp.where(hi == h, low, 0.0) for h in range(TABS)]
        lhs = jnp.concatenate(spread, axis=0).astype(BF16)
        acc = acc + lax.dot_general(
            lhs, hot, (((1,), (1,)), ((), ())), preferred_element_type=F32
        )
    sums = acc[: 8 * TABS] + acc[8 * TABS :]
    d_ref[...] = jnp.zeros_like(d_ref)
    for a in range(PA):
        add_row(d_ref, a * PLANE, sums[16 * a : 16 * a + 8])
        add_row(d_ref, a * PLANE + 9 * PC, sums[16 * a + 8 : 16 * a + 16])
    lane = lane_iota()
    extra = sums[96:104]
    by_col = {}
    for k, flat in enumerate(EXTRAS):
        by_col.setdefault(flat // LANES, []).append((k, flat % LANES))
    for col, entries in by_col.items():
        val = d_ref[:, col * LANES : (col + 1) * LANES]
        for k, at in entries:
            val = val + jnp.where(lane == at, extra[:, k : k + 1], 0.0)
        d_ref[:, col * LANES : (col + 1) * LANES] = val

    for c in range(3):
        x_ref[c : c + 1, :CP] = disp_ref[c] + 0.5 * mesh_ref[c]
    x_ref[3:8, :CP] = jnp.zeros((5, CP), F32)
    x_ref[:, COLS * LANES :] = jnp.zeros((8, LANES), F32)
    top = lax.broadcasted_iota(jnp.int32, (8, LANES), 0) < 3
    for col in range(COLS):
        cut = slice(col * LANES, (col + 1) * LANES)
        d = d_ref[:, cut]
        averaged = d / (2.0 * jnp.maximum(d[3:4], 1.0))
        d_ref[:, cut] = jnp.where(top, averaged + x_ref[:, cut], d + asm_ref[:, cut])
    has_prev = 0.5 * flag_ref[0, 4]
    has_next = 0.5 * flag_ref[0, 5]
    widen(before_ref, wide_ref, 0)
    for col in range(21):
        cut = slice(col * LANES, (col + 1) * LANES)
        val = take_row(wide_ref, LAST_OFF + col * LANES) - x_ref[:, cut]
        d_ref[:, cut] += jnp.where(rim_cut(col) & top, has_prev * val, 0.0)
    widen(after_ref, wide_ref, 0)
    for col in range(21):
        start = LAST_COL * LANES + LAST_OFF + col * LANES
        val = wide_ref[:, col * LANES : (col + 1) * LANES] - take_row(x_ref, start)
        add_row(d_ref, start, jnp.where(rim_cut(col) & top, has_next * val, 0.0))
    for c in range(3):
        new_ref[c] = d_ref[c : c + 1, :CP]
    for c in range(4):
        res_ref[c] = d_ref[4 + c : 5 + c, :CP]


VMEM = pl.BlockSpec(memory_space=pltpu.VMEM)
SMEM = pl.BlockSpec(memory_space=pltpu.SMEM)


def shaped(*shape):
    return jax.ShapeDtypeStruct(shape, F32)


def cost(us):
    return pl.CostEstimate(flops=0, bytes_accessed=int(us * 3.0e6), transcendentals=0)


def call(kernel, outs, n_in, scratch, scalars=(), us=5):
    return pl.pallas_call(
        kernel,
        out_shape=outs,
        in_specs=[SMEM if k in scalars else VMEM for k in range(n_in)],
        out_specs=jax.tree.map(lambda _: VMEM, outs),
        scratch_shapes=[pltpu.VMEM(shape, F32) for shape in scratch],
        compiler_params=pltpu.CompilerParams(vmem_limit_bytes=48 << 20),
        cost_estimate=cost(us),
    )


def shift(shard, axis, by):
    count = lax.axis_size(axis)
    pairs = [(i, i + by) for i in range(count) if 0 <= i + by < count]
    return lax.ppermute(shard, axis, pairs)


def shards(state, mesh_vel, disp, elem_size, live_slabs, trace_rows, penalty):
    rows = trace_rows.reshape(4, SLOTS)
    gammas = penalty.reshape(4, SLOTS)
    groups = lax.axis_size("group")
    group = lax.axis_index("group")
    dom = lax.axis_index("dom")
    stride = groups // 2
    offsets = (1, -1, stride, -stride)
    flags = [(group + step >= 0) & (group + step < groups) for step in offsets]
    flags += [dom > 0, dom < lax.axis_size("dom") - 1, dom < 0, dom < 0]
    flags = jnp.stack(flags).astype(F32).reshape(1, 8)

    own, first, last = call(
        trace_kernel,
        (shaped(4, 8, SLOTS), shaped(4, RIM), shaped(4, RIM)),
        4,
        [(8, WIDE), (8 * TABS, LANES)],
        us=5,
    )(state, mesh_vel, disp, rows)
    partners = [shift(own[k ^ 1], "group", -step) for k, step in enumerate(offsets)]
    moved_before = shift(last, "dom", 1)
    moved_after = shift(first, "dom", -1)

    local, first, last = call(
        element_kernel,
        (shaped(8, WIDE), shaped(4, RIM), shaped(4, RIM)),
        4,
        [
            (8, WIDE),
            (6, 8 * ROWS, LANES),
            (PA, 9, 15, 8, LANES),
            (PA, 9, 12, 8, LANES),
            (SLABS, 8, LANES),
        ],
        scalars=(0,),
        us=15,
    )(live_slabs, state, mesh_vel, elem_size)
    before = shift(last, "dom", 1)
    after = shift(first, "dom", -1)
    assembled, own2 = call(
        assemble_kernel,
        (shaped(8, WIDE), shaped(4, 4, SLOTS)),
        4,
        [(8, RIM + LANES), (8 * TABS, LANES)],
        us=5,
    )(local, before, after, rows)
    reactions = [shift(own2[k ^ 1], "group", -step) for k, step in enumerate(offsets)]
    residual, new_disp = call(
        finish_kernel,
        (shaped(4, 1, CP), shaped(3, 1, CP)),
        18,
        [(8, WIDE), (8, WIDE), (8, RIM + LANES), (8, SLOTS)],
        scalars=(0,),
        us=8,
    )(flags, assembled, mesh_vel, disp, rows, gammas, own, own2, *partners, *reactions, moved_before, moved_after)
    return residual, new_disp


def solution(mesh):
    return jax.shard_map(
        shards,
        mesh=mesh,
        in_specs=(
            P(None, "group", "dom"),
            P(None, "group", "dom"),
            P(None, "group", "dom"),
            P("group", "dom"),
            P("group", "dom"),
            P("group", "dom", None, None),
            P("group", "dom", None, None),
        ),
        out_specs=(P(None, "group", "dom"), P(None, "group", "dom")),
        check_vma=False,
    )
```

```python
import math

import jax
import jax.numpy as jnp
from jax import lax
from jax.experimental import pallas as pl
from jax.experimental.pallas import tpu as pltpu
from jax.sharding import PartitionSpec as P

PA = 6
PB = 10
PC = 130
CP = PA * PB * PC
SLABS = 4
ROWS = PA * PB
PLANE = PB * PC
LANES = 128
COLS = 61
WIDE = (COLS + 1) * LANES
SLOTS = 1024
SHARED = 2 * PLANE
RIM = 21 * LANES
LAST_COL = 4 * PLANE // LANES
LAST_OFF = 4 * PLANE % LANES
TABS = 14

DT = 0.5
NU = 0.05
S = math.sqrt(0.15)
W_EDGE = 5.0 / 18.0
W_MID = 8.0 / 18.0
F32 = jnp.float32
BF16 = jnp.bfloat16


def face_extras():
    out = []
    for a in range(PA):
        base = a * PLANE
        out += [base + b * PC + 129 for b in range(PB)]
        out += [base + 128, base + 9 * PC + 128]
        out += [base + b * PC for b in range(1, PB - 1)]
    return out


EXTRAS = face_extras()


def lane_iota():
    return lax.broadcasted_iota(jnp.int32, (8, LANES), 1)


def take_row(ref, start):
    off = start % LANES
    col = start - off
    first = ref[:, col : col + LANES]
    if off == 0:
        return first
    second = ref[:, col + LANES : col + 2 * LANES]
    mixed = jnp.where(lane_iota() >= off, first, second)
    return pltpu.roll(mixed, LANES - off, 1)


def add_row(ref, start, val):
    off = start % LANES
    col = start - off
    if off == 0:
        ref[:, col : col + LANES] += val
        return
    turned = pltpu.roll(val, off, 1)
    lane = lane_iota()
    ref[:, col : col + LANES] += jnp.where(lane >= off, turned, 0.0)
    ref[:, col + LANES : col + 2 * LANES] += jnp.where(lane < off, turned, 0.0)


def locate(row):
    plane = jnp.zeros_like(row)
    for k in range(1, PA):
        plane = plane + (row >= k * PLANE).astype(jnp.int32)
    rest = row - plane * PLANE
    along_b = jnp.zeros_like(row)
    for k in range(1, PB):
        along_b = along_b + (rest >= k * PC).astype(jnp.int32)
    along_c = rest - along_b * PC
    top = along_b == PB - 1
    straight = ((along_b == 0) | top) & (along_c < LANES)
    which = jnp.where(
        along_c == 129,
        along_b,
        jnp.where(along_c == 128, jnp.where(top, 11, 10), 11 + along_b),
    )
    hi = jnp.where(straight, 2 * plane + top.astype(jnp.int32), 12)
    lo = jnp.where(straight, along_c, 20 * plane + which)
    return hi, lo


def one_hot(lo):
    return (lax.broadcasted_iota(jnp.int32, (LANES, SLOTS), 0) == lo).astype(F32).astype(BF16)


def split_bf16(val):
    high = val.astype(BF16)
    low = (val - high.astype(F32)).astype(BF16)
    return high, low


def face_tables(x_ref, tab_ref):
    lane = lane_iota()
    for a in range(PA):
        tab_ref[16 * a : 16 * a + 8, :] = take_row(x_ref, a * PLANE)
        tab_ref[16 * a + 8 : 16 * a + 16, :] = take_row(x_ref, a * PLANE + 9 * PC)
    extra = jnp.zeros((8, LANES), F32)
    for k, flat in enumerate(EXTRAS):
        extra = jnp.where(lane == k, x_ref[:, flat : flat + 1], extra)
    tab_ref[96:104, :] = extra
    tab_ref[104:112, :] = jnp.zeros((8, LANES), F32)
    high, low = split_bf16(tab_ref[...])
    return jnp.concatenate([high, low], axis=0)


def gather_slots(table, hi, hot):
    full = jnp.dot(table, hot, preferred_element_type=F32)
    out = jnp.zeros((8, SLOTS), F32)
    for h in range(13):
        piece = full[8 * h : 8 * h + 8] + full[112 + 8 * h : 120 + 8 * h]
        out = jnp.where(hi == h, piece, out)
    return out


def fwd_value(x0, x1, x2):
    even, odd = x0 + x2, x2 - x0
    base = 0.2 * even + 0.6 * x1
    mid = 0.125 * even + 0.75 * x1
    side = (S / 2) * odd
    return (base - side, mid, base + side)


def fwd_slope(x0, x1, x2):
    half = 0.5 * (x2 - x0)
    bend = S * ((x0 + x2) - 2.0 * x1)
    return (half - bend, half, half + bend)


def back_value(y0, y1, y2):
    even, odd = y0 + y2, y2 - y0
    ends = (W_EDGE * 0.2) * even + (W_MID * 0.125) * y1
    side = (W_EDGE * S / 2) * odd
    return (ends - side, (W_EDGE * 0.6) * even + (W_MID * 0.75) * y1, ends + side)


def back_slope(z0, z1, z2):
    turn = (W_EDGE * S) * (z2 - z0)
    half = (0.5 * W_EDGE) * (z0 + z2) + (0.5 * W_MID) * z1
    return (turn - half, -2.0 * turn, turn + half)


def both(value, slope):
    return tuple(v + d for v, d in zip(back_value(*value), back_slope(*slope)))


def strided(start):
    return pl.ds(start, 8, stride=8)


def element_stage(live, x_ref, q_ref, g_ref, acc_ref, h_ref, out_ref):
    for r in range(ROWS):
        taps = [take_row(x_ref, r * PC + s) for s in range(3)]
        for k, val in enumerate(fwd_value(*taps) + fwd_slope(*taps)):
            q_ref[k, 8 * r : 8 * r + 8, :] = val

    def along_b(a, carry):
        for f in range(7):
            for qc in range(3):
                value = [q_ref[qc, strided(a * 80 + 8 * s + f), :] for s in range(3)]
                if f >= 4:
                    for qb, val in enumerate(fwd_value(*value)):
                        g_ref[a, 3 * qb + qc, 8 + f] = val
                    continue
                slope = [q_ref[3 + qc, strided(a * 80 + 8 * s + f), :] for s in range(3)]
                vv = fwd_value(*value)
                dv = fwd_slope(*value)
                vd = fwd_value(*slope)
                for qb in range(3):
                    g_ref[a, 3 * qb + qc, 3 * f] = vv[qb]
                    g_ref[a, 3 * qb + qc, 3 * f + 1] = dv[qb]
                    g_ref[a, 3 * qb + qc, 3 * f + 2] = vd[qb]
        return carry

    lax.fori_loop(0, PA, along_b, 0)

    zero = jnp.zeros((8, LANES), F32)

    def clear(a, carry):
        for q in range(9):
            for k in range(12):
                acc_ref[a, q, k] = zero
        return carry

    lax.fori_loop(0, PA, clear, 0)

    def points(slab, q):
        h = h_ref[slab]
        outer = jnp.where(live > slab, h, 0.0)

        def taps(slot):
            return [g_ref[slab + s, q, slot] for s in range(3)]

        grads = [
            [fwd_slope(*taps(3 * f)), fwd_value(*taps(3 * f + 1)), fwd_value(*taps(3 * f + 2))]
            for f in range(4)
        ]
        pressure = fwd_value(*taps(9))
        adv = [fwd_value(*taps(12 + c)) for c in range(3)]
        inv = 1.0 / h
        inv2 = inv * inv
        four = 4.0 * inv2
        fixed = 4.0 / DT**2 + (36.0 * NU**2) * (inv2 * inv2)
        h2 = (h * h) * (1.0 / 12.0)
        coef_f = [[None] * 3 for _ in range(4)]
        coef_k = [[[None] * 3 for _ in range(4)] for _ in range(3)]
        for t in range(3):
            a = [adv[c][t] for c in range(3)]
            conv = [
                a[0] * grads[c][0][t] + a[1] * grads[c][1][t] + a[2] * grads[c][2][t]
                for c in range(3)
            ]
            mom = [conv[c] + grads[3][c][t] for c in range(3)]
            cont = grads[0][0][t] + grads[1][1][t] + grads[2][2][t]
            total = fixed + four * (a[0] * a[0] + a[1] * a[1] + a[2] * a[2])
            tau = lax.rsqrt(total)
            press = h * pressure[t] - h2 * (total * tau) * cont
            scaled = [tau * mom[c] for c in range(3)]
            for c in range(3):
                coef_f[c][t] = h * conv[c]
                coef_k[c][3][t] = scaled[c]
                for d in range(3):
                    val = NU * grads[c][d][t] + a[d] * scaled[c]
                    coef_k[d][c][t] = val - press if d == c else val
            coef_f[3][t] = h * cont
        for c in range(4):
            parts = (
                both(coef_f[c], coef_k[0][c]),
                back_value(*coef_k[1][c]),
                back_value(*coef_k[2][c]),
            )
            for k, part in enumerate(parts):
                for s in range(3):
                    acc_ref[slab + s, q, 3 * c + k] += outer * part[s]

    def slab_loop(slab, carry):
        def point_loop(q, inner):
            points(slab, q)
            return inner

        return lax.fori_loop(0, 9, point_loop, carry)

    lax.fori_loop(0, SLABS, slab_loop, 0)

    def clear_rows(r, carry):
        for k in range(6):
            q_ref[k, pl.ds(pl.multiple_of(r * 8, 8), 8), :] = zero
        return carry

    lax.fori_loop(0, ROWS, clear_rows, 0)

    def back_b(a, carry):
        for c in range(4):
            for qc in range(3):
                pieces = [
                    [acc_ref[a, 3 * qb + qc, 3 * c + k] for qb in range(3)] for k in range(3)
                ]
                straight = both(pieces[0], pieces[1])
                sloped = back_value(*pieces[2])
                for s in range(3):
                    at = strided(a * 80 + 8 * s + 4 + c)
                    q_ref[qc, at, :] += straight[s]
                    q_ref[3 + qc, at, :] += sloped[s]
        return carry

    lax.fori_loop(0, PA, back_b, 0)

    lane = lane_iota()
    pending = zero
    for r in range(ROWS):
        y = [q_ref[k, 8 * r : 8 * r + 8, :] for k in range(6)]
        y0, y1, y2 = both(y[:3], y[3:])
        y1 = pltpu.roll(y1, 1, 1)
        y2 = pltpu.roll(y2, 2, 1)
        main = y0 + jnp.where(lane >= 1, y1, 0.0) + jnp.where(lane >= 2, y2, 0.0)
        tail = jnp.where(lane < 1, y1, 0.0) + jnp.where(lane < 2, y2, 0.0)
        off = 2 * r
        if off:
            main = pltpu.roll(main, off, 1)
            tail = pltpu.roll(tail, off, 1)
        out_ref[:, r * LANES : (r + 1) * LANES] = jnp.where(lane >= off, main, pending)
        pending = jnp.where(lane < off, main, tail)
    out_ref[:, ROWS * LANES : (ROWS + 1) * LANES] = pending
    out_ref[:, COLS * LANES :] = zero


def rim_cut(col):
    return lane_iota() < min(LANES, SHARED - col * LANES)


def widen(rim_ref, wide_ref, low):
    wide_ref[...] = jnp.zeros_like(wide_ref)
    wide_ref[low : low + 4, :RIM] = rim_ref[...]


def cut_rims(x_ref, low, rim_ref):
    rim_ref[0] = x_ref[low : low + 4, :RIM]
    rim_ref[1] = x_ref[low : low + 4, LAST_COL * LANES : LAST_COL * LANES + RIM]


def main_kernel(
    live_hbm, state_hbm, mesh_hbm, disp_hbm, size_hbm, rows_hbm, pen_hbm,
    base_ref, term_ref,
    live_ref, state_ref, mesh_ref, disp_ref, size_ref, rows_ref, pen_ref, x_ref, f_ref, q_ref, g_ref, acc_ref, h_ref, tab_ref, wide_ref,
    own_ref, part_ref, own2_ref, part2_ref, rim_ref, rim_in_ref, rim2_ref, rim2_in_ref,
    load_sem, send_sem, recv_sem,
):
    groups = lax.axis_size("group")
    doms = lax.axis_size("dom")
    group = lax.axis_index("group")
    dom = lax.axis_index("dom")
    stride = groups // 2
    offsets = (1, -1, stride, -stride)
    slots = [
        (group + step, dom, (group + step >= 0) & (group + step < groups)) for step in offsets
    ]
    sides = [(group, dom - 1, dom > 0), (group, dom + 1, dom < doms - 1)]
    loads = []
    for src, dst, count in ((state_hbm, state_ref, 4), (mesh_hbm, mesh_ref, 3), (disp_hbm, disp_ref, 3)):
        for c in range(count):
            loads.append(
                pltpu.make_async_copy(src.at[c], dst.at[c], load_sem.at[len(loads)])
            )
    small = (
        (live_hbm, live_ref),
        (size_hbm, size_ref),
        (rows_hbm.at[0, 0], rows_ref),
        (pen_hbm.at[0, 0], pen_ref),
    )
    for src, dst in small:
        loads.append(pltpu.make_async_copy(src, dst, load_sem.at[len(loads)]))
    for load in loads:
        load.start()

    barrier = pltpu.get_barrier_semaphore()
    peers = 0
    for to_group, to_dom, present in slots + sides:
        peers = peers + present.astype(jnp.int32)

        @pl.when(present)
        def _():
            pl.semaphore_signal(
                barrier, inc=1, device_id=(to_group, to_dom), device_id_type=pl.DeviceIdType.MESH
            )

    def remote(src, dst, at, to, arrive):
        return pltpu.make_async_remote_copy(
            src_ref=src,
            dst_ref=dst,
            send_sem=send_sem.at[at],
            recv_sem=recv_sem.at[arrive],
            device_id=(to[0], to[1]),
            device_id_type=pl.DeviceIdType.MESH,
        )

    def exchange(out_ref, in_ref, peers_of, sem):
        return [
            (to[2], remote(out_ref.at[k], in_ref.at[k ^ 1], sem + k, to, sem + (k ^ 1)),
             remote(out_ref.at[k], in_ref.at[k], sem + k, to, sem + k))
            for k, to in enumerate(peers_of)
        ]

    def launch(copies):
        for present, out, _ in copies:

            @pl.when(present)
            def _():
                out.start()

    def land(copies):
        for present, _, back in copies:

            @pl.when(present)
            def _():
                back.wait_recv()

    def drain(copies):
        for present, out, _ in copies:

            @pl.when(present)
            def _():
                out.wait_send()

    traces = exchange(own_ref, part_ref, slots, 0)
    traces2 = exchange(own2_ref, part2_ref, slots, 4)
    rims = exchange(rim_ref, rim_in_ref, sides, 8)
    rims2 = exchange(rim2_ref, rim2_in_ref, sides, 10)

    for load in loads:
        load.wait()
    for c in range(3):
        x_ref[c : c + 1, :CP] = disp_ref[c] + 0.5 * mesh_ref[c]
        f_ref[4 + c : 5 + c, :CP] = state_ref[c] - mesh_ref[c]
    x_ref[3:4, :CP] = jnp.zeros((1, CP), F32)
    f_ref[7:8, :CP] = jnp.zeros((1, CP), F32)
    for c in range(4):
        x_ref[4 + c : 5 + c, :CP] = state_ref[c]
        f_ref[c : c + 1, :CP] = state_ref[c]
    x_ref[:, COLS * LANES :] = jnp.zeros((8, LANES), F32)
    f_ref[:, COLS * LANES :] = jnp.zeros((8, LANES), F32)
    for k in range(32):
        h_ref[k // 8, k % 8 : k % 8 + 1, :] = size_ref[:, k * LANES : (k + 1) * LANES]
    cut_rims(x_ref, 0, rim_ref)
    table = face_tables(x_ref, tab_ref)
    for k in range(4):
        hi, lo = locate(rows_ref[k : k + 1, :])
        own_ref[k] = gather_slots(table, hi, one_hot(lo))

    pl.semaphore_wait(barrier, peers)
    launch(rims)
    launch(traces)

    live = jnp.broadcast_to(live_ref[...], (8, LANES))
    element_stage(live, f_ref, q_ref, g_ref, acc_ref, h_ref, base_ref)
    cut_rims(base_ref, 4, rim2_ref)
    launch(rims2)

    for k, (_, _, present) in enumerate(slots):

        @pl.when(jnp.logical_not(present))
        def _():
            part_ref[k] = jnp.zeros((8, SLOTS), F32)
            part2_ref[k] = jnp.zeros((4, SLOTS), F32)

    for k, (_, _, present) in enumerate(sides):

        @pl.when(jnp.logical_not(present))
        def _():
            rim_in_ref[k] = jnp.zeros((4, RIM), F32)
            rim2_in_ref[k] = jnp.zeros((4, RIM), F32)

    land(rims)
    has_prev = 0.5 * sides[0][2].astype(F32)
    has_next = 0.5 * sides[1][2].astype(F32)
    top = lax.broadcasted_iota(jnp.int32, (8, LANES), 0) < 3
    for col in range(COLS):
        cut = slice(col * LANES, (col + 1) * LANES)
        base_ref[:, cut] = jnp.where(top, x_ref[:, cut], base_ref[:, cut])
    widen(rim_in_ref.at[0], wide_ref, 0)
    for col in range(21):
        cut = slice(col * LANES, (col + 1) * LANES)
        val = take_row(wide_ref, LAST_OFF + col * LANES) - x_ref[:, cut]
        base_ref[:, cut] += jnp.where(rim_cut(col) & top, has_prev * val, 0.0)
    widen(rim_in_ref.at[1], wide_ref, 0)
    for col in range(21):
        start = LAST_COL * LANES + LAST_OFF + col * LANES
        val = wide_ref[:, col * LANES : (col + 1) * LANES] - take_row(x_ref, start)
        add_row(base_ref, start, jnp.where(rim_cut(col) & top, has_next * val, 0.0))

    land(rims2)
    widen(rim2_in_ref.at[0], wide_ref, 4)
    for col in range(21):
        val = jnp.where(rim_cut(col), take_row(wide_ref, LAST_OFF + col * LANES), 0.0)
        base_ref[:, col * LANES : (col + 1) * LANES] += val
    widen(rim2_in_ref.at[1], wide_ref, 4)
    for col in range(21):
        val = jnp.where(rim_cut(col), wide_ref[:, col * LANES : (col + 1) * LANES], 0.0)
        add_row(base_ref, LAST_COL * LANES + LAST_OFF + col * LANES, val)
    table = face_tables(base_ref, tab_ref)
    for k in range(4):
        hi, lo = locate(rows_ref[k : k + 1, :])
        own2_ref[k] = gather_slots(table, hi, one_hot(lo))[4:8]
    launch(traces2)

    land(traces)
    for k, (_, _, present) in enumerate(slots):
        live_slot = present.astype(F32)
        gap = (part_ref[k] - own_ref[k]) * live_slot
        term_ref[k] = gap
        term_ref[k, 3:4, :] = jnp.zeros((1, SLOTS), F32) + live_slot
        term_ref[k, 4:8, :] = -pen_ref[k : k + 1, :] * gap[4:8]
    land(traces2)
    for k, (_, _, present) in enumerate(slots):
        half = 0.5 * present.astype(F32)
        term_ref[k, 4:8, :] += half * (part2_ref[k] - own2_ref[k])
    for copies in (rims, traces, rims2, traces2):
        drain(copies)


def finish_kernel(base_ref, term_in_ref, rows_ref, res_ref, new_ref, d_ref):
    acc = jnp.zeros((2 * 8 * TABS, LANES), F32)
    for k in range(4):
        term = term_in_ref[k]
        hi, lo = locate(rows_ref[k : k + 1, :])
        hot = one_hot(lo)
        high = term.astype(BF16).astype(F32)
        low = term - high
        spread = [jnp.where(hi == h, high, 0.0) for h in range(TABS)]
        spread += [jnp.where(hi == h, low, 0.0) for h in range(TABS)]
        lhs = jnp.concatenate(spread, axis=0).astype(BF16)
        acc = acc + lax.dot_general(
            lhs, hot, (((1,), (1,)), ((), ())), preferred_element_type=F32
        )
    sums = acc[: 8 * TABS] + acc[8 * TABS :]
    d_ref[...] = jnp.zeros_like(d_ref)
    for a in range(PA):
        add_row(d_ref, a * PLANE, sums[16 * a : 16 * a + 8])
        add_row(d_ref, a * PLANE + 9 * PC, sums[16 * a + 8 : 16 * a + 16])
    lane = lane_iota()
    extra = sums[96:104]
    by_col = {}
    for k, flat in enumerate(EXTRAS):
        by_col.setdefault(flat // LANES, []).append((k, flat % LANES))
    for col, entries in by_col.items():
        val = d_ref[:, col * LANES : (col + 1) * LANES]
        for k, at in entries:
            val = val + jnp.where(lane == at, extra[:, k : k + 1], 0.0)
        d_ref[:, col * LANES : (col + 1) * LANES] = val
    top = lax.broadcasted_iota(jnp.int32, (8, LANES), 0) < 3
    for col in range(COLS):
        cut = slice(col * LANES, (col + 1) * LANES)
        d = d_ref[:, cut]
        averaged = d / (2.0 * jnp.maximum(d[3:4], 1.0))
        d_ref[:, cut] = jnp.where(top, averaged, d) + base_ref[:, cut]
    for c in range(3):
        new_ref[c] = d_ref[c : c + 1, :CP]
    for c in range(4):
        res_ref[c] = d_ref[4 + c : 5 + c, :CP]


VMEM = pl.BlockSpec(memory_space=pltpu.VMEM)
HBM = pl.BlockSpec(memory_space=pltpu.HBM)


def shaped(*shape):
    return jax.ShapeDtypeStruct(shape, F32)


def shards(state, mesh_vel, disp, elem_size, live_slabs, trace_rows, penalty):
    rows = trace_rows.reshape(4, SLOTS)
    base, terms = pl.pallas_call(
        main_kernel,
        out_shape=(shaped(8, WIDE), shaped(4, 8, SLOTS)),
        in_specs=[HBM] * 7,
        out_specs=(VMEM, VMEM),
        scratch_shapes=[
            pltpu.VMEM((1, 1), jnp.int32),
            pltpu.VMEM((4, 1, CP), F32),
            pltpu.VMEM((3, 1, CP), F32),
            pltpu.VMEM((3, 1, CP), F32),
            pltpu.VMEM((1, SLABS * SLOTS), F32),
            pltpu.VMEM((4, SLOTS), jnp.int32),
            pltpu.VMEM((4, SLOTS), F32),
            pltpu.VMEM((8, WIDE), F32),
            pltpu.VMEM((8, WIDE), F32),
            pltpu.VMEM((6, 8 * ROWS, LANES), F32),
            pltpu.VMEM((PA, 9, 15, 8, LANES), F32),
            pltpu.VMEM((PA, 9, 12, 8, LANES), F32),
            pltpu.VMEM((SLABS, 8, LANES), F32),
            pltpu.VMEM((8 * TABS, LANES), F32),
            pltpu.VMEM((8, RIM + LANES), F32),
            pltpu.VMEM((4, 8, SLOTS), F32),
            pltpu.VMEM((4, 8, SLOTS), F32),
            pltpu.VMEM((4, 4, SLOTS), F32),
            pltpu.VMEM((4, 4, SLOTS), F32),
            pltpu.VMEM((2, 4, RIM), F32),
            pltpu.VMEM((2, 4, RIM), F32),
            pltpu.VMEM((2, 4, RIM), F32),
            pltpu.VMEM((2, 4, RIM), F32),
            pltpu.SemaphoreType.DMA((14,)),
            pltpu.SemaphoreType.DMA((12,)),
            pltpu.SemaphoreType.DMA((12,)),
        ],
        compiler_params=pltpu.CompilerParams(
            vmem_limit_bytes=48 << 20, collective_id=0, has_side_effects=True
        ),
    )(live_slabs, state, mesh_vel, disp, elem_size, trace_rows, penalty)
    return pl.pallas_call(
        finish_kernel,
        out_shape=(shaped(4, 1, CP), shaped(3, 1, CP)),
        in_specs=[VMEM] * 3,
        out_specs=(VMEM, VMEM),
        scratch_shapes=[pltpu.VMEM((8, WIDE), F32)],
        compiler_params=pltpu.CompilerParams(vmem_limit_bytes=16 << 20),
    )(base, terms, rows)


def solution(mesh):
    return jax.shard_map(
        shards,
        mesh=mesh,
        in_specs=(
            P(None, "group", "dom"),
            P(None, "group", "dom"),
            P(None, "group", "dom"),
            P("group", "dom"),
            P("group", "dom"),
            P("group", "dom", None, None),
            P("group", "dom", None, None),
        ),
        out_specs=(P(None, "group", "dom"), P(None, "group", "dom")),
        check_vma=False,
    )
```

```python
import math

import jax
import jax.numpy as jnp
from jax import lax
from jax.experimental import pallas as pl
from jax.experimental.pallas import tpu as pltpu
from jax.sharding import PartitionSpec as P

PA = 6
PB = 10
PC = 130
CP = PA * PB * PC
SLABS = 4
ROWS = PA * PB
PLANE = PB * PC
LANES = 128
COLS = 61
WIDE = (COLS + 1) * LANES
SLOTS = 1024
SHARED = 2 * PLANE
RIM = 21 * LANES
LAST_COL = 4 * PLANE // LANES
LAST_OFF = 4 * PLANE % LANES
TABS = 14

DT = 0.5
NU = 0.05
S = math.sqrt(0.15)
W_EDGE = 5.0 / 18.0
W_MID = 8.0 / 18.0
F32 = jnp.float32
BF16 = jnp.bfloat16


def face_extras():
    out = []
    for a in range(PA):
        base = a * PLANE
        out += [base + b * PC + 129 for b in range(PB)]
        out += [base + 128, base + 9 * PC + 128]
        out += [base + b * PC for b in range(1, PB - 1)]
    return out


EXTRAS = face_extras()


def lane_iota():
    return lax.broadcasted_iota(jnp.int32, (8, LANES), 1)


def take_row(ref, start):
    off = start % LANES
    col = start - off
    first = ref[:, col : col + LANES]
    if off == 0:
        return first
    second = ref[:, col + LANES : col + 2 * LANES]
    mixed = jnp.where(lane_iota() >= off, first, second)
    return pltpu.roll(mixed, LANES - off, 1)


def add_row(ref, start, val):
    off = start % LANES
    col = start - off
    if off == 0:
        ref[:, col : col + LANES] += val
        return
    turned = pltpu.roll(val, off, 1)
    lane = lane_iota()
    ref[:, col : col + LANES] += jnp.where(lane >= off, turned, 0.0)
    ref[:, col + LANES : col + 2 * LANES] += jnp.where(lane < off, turned, 0.0)


def locate(row):
    plane = jnp.zeros_like(row)
    for k in range(1, PA):
        plane = plane + (row >= k * PLANE).astype(jnp.int32)
    rest = row - plane * PLANE
    along_b = jnp.zeros_like(row)
    for k in range(1, PB):
        along_b = along_b + (rest >= k * PC).astype(jnp.int32)
    along_c = rest - along_b * PC
    top = along_b == PB - 1
    straight = ((along_b == 0) | top) & (along_c < LANES)
    which = jnp.where(
        along_c == 129,
        along_b,
        jnp.where(along_c == 128, jnp.where(top, 11, 10), 11 + along_b),
    )
    hi = jnp.where(straight, 2 * plane + top.astype(jnp.int32), 12)
    lo = jnp.where(straight, along_c, 20 * plane + which)
    return hi, lo


def one_hot(lo):
    return (lax.broadcasted_iota(jnp.int32, (LANES, SLOTS), 0) == lo).astype(F32).astype(BF16)


def split_bf16(val):
    high = val.astype(BF16)
    low = (val - high.astype(F32)).astype(BF16)
    return high, low


def face_extra(x_ref):
    lane = lane_iota()
    extra = jnp.zeros((8, LANES), F32)
    for k, flat in enumerate(EXTRAS):
        extra = jnp.where(lane == k, x_ref[:, flat : flat + 1], extra)
    return extra


def face_tables(x_ref, tab_ref):
    for a in range(PA):
        tab_ref[16 * a : 16 * a + 8, :] = take_row(x_ref, a * PLANE)
        tab_ref[16 * a + 8 : 16 * a + 16, :] = take_row(x_ref, a * PLANE + 9 * PC)
    tab_ref[96:104, :] = face_extra(x_ref)
    tab_ref[104:112, :] = jnp.zeros((8, LANES), F32)
    high, low = split_bf16(tab_ref[...])
    return jnp.concatenate([high, low], axis=0)


def gather_slots(table, hi, hot):
    full = jnp.dot(table, hot, preferred_element_type=F32)
    out = jnp.zeros((8, SLOTS), F32)
    for h in range(13):
        piece = full[8 * h : 8 * h + 8] + full[112 + 8 * h : 120 + 8 * h]
        out = jnp.where(hi == h, piece, out)
    return out


def low_half():
    return lax.broadcasted_iota(jnp.int32, (8, LANES), 0) < 4


def pair_tables(x_ref):
    low = low_half()
    tiles = []
    for a in range(PA):
        front = pltpu.roll(take_row(x_ref, a * PLANE), 4, 0)
        tiles.append(jnp.where(low, front, take_row(x_ref, a * PLANE + 9 * PC)))
    tiles.append(jnp.where(low, pltpu.roll(face_extra(x_ref), 4, 0), 0.0))
    tiles.append(jnp.zeros((8, LANES), F32))
    high, low = split_bf16(jnp.concatenate(tiles, axis=0))
    return jnp.concatenate([high, low], axis=0)


def paired(hi):
    return hi - (lax.broadcasted_iota(jnp.int32, (8, SLOTS), 0) >= 4).astype(jnp.int32)


def gather_pairs(table, hi, hot):
    full = jnp.dot(table, hot, preferred_element_type=F32)
    which = paired(hi)
    out = jnp.zeros((8, SLOTS), F32)
    for p in range(7):
        piece = full[8 * p : 8 * p + 8] + full[64 + 8 * p : 72 + 8 * p]
        out = jnp.where(which == 2 * p, piece, out)
    return out[0:4] + out[4:8]


def scatter_dot(term, which, step, tiles, hot):
    high = term.astype(BF16).astype(F32)
    low = term - high
    spread = [jnp.where(which == step * p, high, 0.0) for p in range(tiles)]
    spread += [jnp.where(which == step * p, low, 0.0) for p in range(tiles)]
    lhs = jnp.concatenate(spread, axis=0).astype(BF16)
    return lax.dot_general(lhs, hot, (((1,), (1,)), ((), ())), preferred_element_type=F32)


def add_extra(d_ref, extra):
    lane = lane_iota()
    by_col = {}
    for k, flat in enumerate(EXTRAS):
        by_col.setdefault(flat // LANES, []).append((k, flat % LANES))
    for col, entries in by_col.items():
        val = d_ref[:, col * LANES : (col + 1) * LANES]
        for k, at in entries:
            val = val + jnp.where(lane == at, extra[:, k : k + 1], 0.0)
        d_ref[:, col * LANES : (col + 1) * LANES] = val


def fwd_value(x0, x1, x2):
    even, odd = x0 + x2, x2 - x0
    base = 0.2 * even + 0.6 * x1
    mid = 0.125 * even + 0.75 * x1
    side = (S / 2) * odd
    return (base - side, mid, base + side)


def fwd_slope(x0, x1, x2):
    half = 0.5 * (x2 - x0)
    bend = S * ((x0 + x2) - 2.0 * x1)
    return (half - bend, half, half + bend)


def back_value(y0, y1, y2):
    even, odd = y0 + y2, y2 - y0
    ends = (W_EDGE * 0.2) * even + (W_MID * 0.125) * y1
    side = (W_EDGE * S / 2) * odd
    return (ends - side, (W_EDGE * 0.6) * even + (W_MID * 0.75) * y1, ends + side)


def back_slope(z0, z1, z2):
    turn = (W_EDGE * S) * (z2 - z0)
    half = (0.5 * W_EDGE) * (z0 + z2) + (0.5 * W_MID) * z1
    return (turn - half, -2.0 * turn, turn + half)


def both(value, slope):
    return tuple(v + d for v, d in zip(back_value(*value), back_slope(*slope)))


def strided(start):
    return pl.ds(start, 8, stride=8)


def element_stage(live, x_ref, q_ref, g_ref, acc_ref, h_ref, out_ref):
    for r in range(ROWS):
        taps = [take_row(x_ref, r * PC + s) for s in range(3)]
        for k, val in enumerate(fwd_value(*taps) + fwd_slope(*taps)):
            q_ref[k, 8 * r : 8 * r + 8, :] = val

    def along_b(a, carry):
        for f in range(7):
            for qc in range(3):
                value = [q_ref[qc, strided(a * 80 + 8 * s + f), :] for s in range(3)]
                if f >= 4:
                    for qb, val in enumerate(fwd_value(*value)):
                        g_ref[a, 3 * qb + qc, 8 + f] = val
                    continue
                slope = [q_ref[3 + qc, strided(a * 80 + 8 * s + f), :] for s in range(3)]
                vv = fwd_value(*value)
                dv = fwd_slope(*value)
                vd = fwd_value(*slope)
                for qb in range(3):
                    g_ref[a, 3 * qb + qc, 3 * f] = vv[qb]
                    g_ref[a, 3 * qb + qc, 3 * f + 1] = dv[qb]
                    g_ref[a, 3 * qb + qc, 3 * f + 2] = vd[qb]
        return carry

    lax.fori_loop(0, PA, along_b, 0)

    zero = jnp.zeros((8, LANES), F32)

    def clear(a, carry):
        for q in range(9):
            for k in range(12):
                acc_ref[a, q, k] = zero
        return carry

    lax.fori_loop(0, 2, clear, 0)

    def points(slab, q):
        h = h_ref[slab]
        outer = jnp.where(live > slab, h, 0.0)

        def taps(slot):
            return [g_ref[slab + s, q, slot] for s in range(3)]

        grads = [
            [fwd_slope(*taps(3 * f)), fwd_value(*taps(3 * f + 1)), fwd_value(*taps(3 * f + 2))]
            for f in range(4)
        ]
        pressure = fwd_value(*taps(9))
        adv = [fwd_value(*taps(12 + c)) for c in range(3)]
        inv = 1.0 / h
        inv2 = inv * inv
        four = 4.0 * inv2
        fixed = 4.0 / DT**2 + (36.0 * NU**2) * (inv2 * inv2)
        h2 = (h * h) * (1.0 / 12.0)
        coef_f = [[None] * 3 for _ in range(4)]
        coef_k = [[[None] * 3 for _ in range(4)] for _ in range(3)]
        for t in range(3):
            a = [adv[c][t] for c in range(3)]
            conv = [
                a[0] * grads[c][0][t] + a[1] * grads[c][1][t] + a[2] * grads[c][2][t]
                for c in range(3)
            ]
            mom = [conv[c] + grads[3][c][t] for c in range(3)]
            cont = grads[0][0][t] + grads[1][1][t] + grads[2][2][t]
            total = fixed + four * (a[0] * a[0] + a[1] * a[1] + a[2] * a[2])
            tau = lax.rsqrt(total)
            press = h * pressure[t] - h2 * (total * tau) * cont
            scaled = [tau * mom[c] for c in range(3)]
            for c in range(3):
                coef_f[c][t] = h * conv[c]
                coef_k[c][3][t] = scaled[c]
                for d in range(3):
                    val = NU * grads[c][d][t] + a[d] * scaled[c]
                    coef_k[d][c][t] = val - press if d == c else val
            coef_f[3][t] = h * cont
        for c in range(4):
            parts = (
                both(coef_f[c], coef_k[0][c]),
                back_value(*coef_k[1][c]),
                back_value(*coef_k[2][c]),
            )
            for k, part in enumerate(parts):
                for s in range(2):
                    acc_ref[slab + s, q, 3 * c + k] += outer * part[s]
                acc_ref[slab + 2, q, 3 * c + k] = outer * part[2]

    def slab_loop(slab, carry):
        def point_loop(q, inner):
            points(slab, q)
            return inner

        return lax.fori_loop(0, 9, point_loop, carry)

    lax.fori_loop(0, SLABS, slab_loop, 0)

    for a in range(PA):
        for k in range(6):
            q_ref[k, a * 80 + 64 : a * 80 + 72, :] = zero
            q_ref[k, a * 80 + 72 : a * 80 + 80, :] = zero

    def back_b(a, carry):
        for c in range(4):
            for qc in range(3):
                pieces = [
                    [acc_ref[a, 3 * qb + qc, 3 * c + k] for qb in range(3)] for k in range(3)
                ]
                straight = both(pieces[0], pieces[1])
                sloped = back_value(*pieces[2])
                at = strided(a * 80 + 4 + c)
                q_ref[qc, at, :] = straight[0]
                q_ref[3 + qc, at, :] = sloped[0]
                for s in range(1, 3):
                    at = strided(a * 80 + 8 * s + 4 + c)
                    q_ref[qc, at, :] += straight[s]
                    q_ref[3 + qc, at, :] += sloped[s]
        return carry

    lax.fori_loop(0, PA, back_b, 0)

    lane = lane_iota()
    pending = zero
    for r in range(ROWS):
        y = [q_ref[k, 8 * r : 8 * r + 8, :] for k in range(6)]
        y0, y1, y2 = both(y[:3], y[3:])
        y1 = pltpu.roll(y1, 1, 1)
        y2 = pltpu.roll(y2, 2, 1)
        main = y0 + jnp.where(lane >= 1, y1, 0.0) + jnp.where(lane >= 2, y2, 0.0)
        tail = jnp.where(lane < 1, y1, 0.0) + jnp.where(lane < 2, y2, 0.0)
        off = 2 * r
        if off:
            main = pltpu.roll(main, off, 1)
            tail = pltpu.roll(tail, off, 1)
        out_ref[:, r * LANES : (r + 1) * LANES] = jnp.where(lane >= off, main, pending)
        pending = jnp.where(lane < off, main, tail)
    out_ref[:, ROWS * LANES : (ROWS + 1) * LANES] = pending
    out_ref[:, COLS * LANES :] = zero


def rim_cut(col):
    return lane_iota() < min(LANES, SHARED - col * LANES)


def widen(rim_ref, wide_ref, low):
    wide_ref[...] = jnp.zeros_like(wide_ref)
    wide_ref[low : low + 4, :RIM] = rim_ref[...]


def cut_rims(x_ref, low, rim_ref):
    rim_ref[0] = x_ref[low : low + 4, :RIM]
    rim_ref[1] = x_ref[low : low + 4, LAST_COL * LANES : LAST_COL * LANES + RIM]


def main_kernel(
    live_ref, state_hbm, mesh_hbm, disp_hbm, size_hbm, rows_hbm, pen_hbm,
    base_ref,
    state_ref, mesh_ref, disp_ref, size_ref, rows_ref, pen_ref, x_ref, f_ref, q_ref, g_ref, acc_ref, h_ref, tab_ref, wide_ref,
    own_ref, part_ref, own2_ref, part2_ref, rim_ref, rim_in_ref, rim2_ref, rim2_in_ref,
    hot_ref, hi_ref, d_ref, term_ref, load_sem, send_sem, recv_sem,
):
    groups = lax.axis_size("group")
    doms = lax.axis_size("dom")
    group = lax.axis_index("group")
    dom = lax.axis_index("dom")
    stride = groups // 2
    offsets = (1, -1, stride, -stride)
    slots = [
        (group + step, dom, (group + step >= 0) & (group + step < groups)) for step in offsets
    ]
    sides = [(group, dom - 1, dom > 0), (group, dom + 1, dom < doms - 1)]
    loads = []
    for src, dst, count in ((state_hbm, state_ref, 4), (mesh_hbm, mesh_ref, 3), (disp_hbm, disp_ref, 3)):
        for c in range(count):
            loads.append(
                pltpu.make_async_copy(src.at[c], dst.at[c], load_sem.at[len(loads)])
            )
    small = (
        (size_hbm, size_ref),
        (rows_hbm.at[0, 0], rows_ref),
        (pen_hbm.at[0, 0], pen_ref),
    )
    for src, dst in small:
        loads.append(pltpu.make_async_copy(src, dst, load_sem.at[len(loads)]))
    for load in loads:
        load.start()

    barrier = pltpu.get_barrier_semaphore()
    peers = 0
    for to_group, to_dom, present in slots + sides:
        peers = peers + present.astype(jnp.int32)

        @pl.when(present)
        def _():
            pl.semaphore_signal(
                barrier, inc=1, device_id=(to_group, to_dom), device_id_type=pl.DeviceIdType.MESH
            )

    def remote(src, dst, at, to, arrive):
        return pltpu.make_async_remote_copy(
            src_ref=src,
            dst_ref=dst,
            send_sem=send_sem.at[at],
            recv_sem=recv_sem.at[arrive],
            device_id=(to[0], to[1]),
            device_id_type=pl.DeviceIdType.MESH,
        )

    def exchange(out_ref, in_ref, peers_of, sem):
        return [
            (to[2], remote(out_ref.at[k], in_ref.at[k ^ 1], sem + k, to, sem + (k ^ 1)),
             remote(out_ref.at[k], in_ref.at[k], sem + k, to, sem + k))
            for k, to in enumerate(peers_of)
        ]

    def launch(copies):
        for present, out, _ in copies:

            @pl.when(present)
            def _():
                out.start()

    def land(copies):
        for present, _, back in copies:

            @pl.when(present)
            def _():
                back.wait_recv()

    def drain(copies):
        for present, out, _ in copies:

            @pl.when(present)
            def _():
                out.wait_send()

    traces = exchange(own_ref, part_ref, slots, 0)
    traces2 = exchange(own2_ref, part2_ref, slots, 4)
    rims = exchange(rim_ref, rim_in_ref, sides, 8)
    rims2 = exchange(rim2_ref, rim2_in_ref, sides, 10)

    for load in loads:
        load.wait()
    for c in range(3):
        x_ref[c : c + 1, :CP] = disp_ref[c] + 0.5 * mesh_ref[c]
        f_ref[4 + c : 5 + c, :CP] = state_ref[c] - mesh_ref[c]
    x_ref[3:4, :CP] = jnp.zeros((1, CP), F32)
    f_ref[7:8, :CP] = jnp.zeros((1, CP), F32)
    for c in range(4):
        x_ref[4 + c : 5 + c, :CP] = state_ref[c]
        f_ref[c : c + 1, :CP] = state_ref[c]
    x_ref[:, COLS * LANES :] = jnp.zeros((8, LANES), F32)
    f_ref[:, COLS * LANES :] = jnp.zeros((8, LANES), F32)
    for k in range(32):
        h_ref[k // 8, k % 8 : k % 8 + 1, :] = size_ref[:, k * LANES : (k + 1) * LANES]
    cut_rims(x_ref, 0, rim_ref)
    table = face_tables(x_ref, tab_ref)
    for k in range(4):
        hi, lo = locate(rows_ref[k : k + 1, :])
        hi_ref[k : k + 1, :] = hi
        hot = one_hot(lo)
        hot_ref[k] = hot
        own_ref[k] = gather_slots(table, hi, hot)

    pl.semaphore_wait(barrier, peers)
    launch(rims)
    launch(traces)

    live = jnp.zeros((8, LANES), jnp.int32) + live_ref[0, 0]
    element_stage(live, f_ref, q_ref, g_ref, acc_ref, h_ref, base_ref)
    cut_rims(base_ref, 4, rim2_ref)
    launch(rims2)

    for k, (_, _, present) in enumerate(slots):

        @pl.when(jnp.logical_not(present))
        def _():
            part_ref[k] = jnp.zeros((8, SLOTS), F32)
            part2_ref[k] = jnp.zeros((4, SLOTS), F32)

    for k, (_, _, present) in enumerate(sides):

        @pl.when(jnp.logical_not(present))
        def _():
            rim_in_ref[k] = jnp.zeros((4, RIM), F32)
            rim2_in_ref[k] = jnp.zeros((4, RIM), F32)

    land(rims)
    has_prev = 0.5 * sides[0][2].astype(F32)
    has_next = 0.5 * sides[1][2].astype(F32)
    top = lax.broadcasted_iota(jnp.int32, (8, LANES), 0) < 3
    for col in range(COLS):
        cut = slice(col * LANES, (col + 1) * LANES)
        base_ref[:, cut] = jnp.where(top, x_ref[:, cut], base_ref[:, cut])
    widen(rim_in_ref.at[0], wide_ref, 0)
    for col in range(21):
        cut = slice(col * LANES, (col + 1) * LANES)
        val = take_row(wide_ref, LAST_OFF + col * LANES) - x_ref[:, cut]
        base_ref[:, cut] += jnp.where(rim_cut(col) & top, has_prev * val, 0.0)
    widen(rim_in_ref.at[1], wide_ref, 0)
    for col in range(21):
        start = LAST_COL * LANES + LAST_OFF + col * LANES
        val = wide_ref[:, col * LANES : (col + 1) * LANES] - take_row(x_ref, start)
        add_row(base_ref, start, jnp.where(rim_cut(col) & top, has_next * val, 0.0))

    land(rims2)
    widen(rim2_in_ref.at[0], wide_ref, 4)
    for col in range(21):
        val = jnp.where(rim_cut(col), take_row(wide_ref, LAST_OFF + col * LANES), 0.0)
        base_ref[:, col * LANES : (col + 1) * LANES] += val
    widen(rim2_in_ref.at[1], wide_ref, 4)
    for col in range(21):
        val = jnp.where(rim_cut(col), wide_ref[:, col * LANES : (col + 1) * LANES], 0.0)
        add_row(base_ref, LAST_COL * LANES + LAST_OFF + col * LANES, val)
    table = pair_tables(base_ref)
    for k in range(4):
        own2_ref[k] = gather_pairs(table, hi_ref[k : k + 1, :], hot_ref[k])
    launch(traces2)

    d_ref[...] = jnp.zeros_like(d_ref)
    land(traces)
    acc = jnp.zeros((2 * 8 * TABS, LANES), F32)
    for k, (_, _, present) in enumerate(slots):
        live_slot = present.astype(F32)
        gap = (part_ref[k] - own_ref[k]) * live_slot
        term_ref[...] = gap
        term_ref[3:4, :] = jnp.zeros((1, SLOTS), F32) + live_slot
        term_ref[4:8, :] = -pen_ref[k : k + 1, :] * gap[4:8] - (0.5 * live_slot) * own2_ref[k]
        acc = acc + scatter_dot(term_ref[...], hi_ref[k : k + 1, :], 1, TABS, hot_ref[k])
    sums = acc[: 8 * TABS] + acc[8 * TABS :]
    for a in range(PA):
        add_row(d_ref, a * PLANE, sums[16 * a : 16 * a + 8])
        add_row(d_ref, a * PLANE + 9 * PC, sums[16 * a + 8 : 16 * a + 16])
    add_extra(d_ref, sums[96:104])
    for col in range(COLS):
        cut = slice(col * LANES, (col + 1) * LANES)
        d = d_ref[:, cut]
        averaged = d / (2.0 * jnp.maximum(d[3:4], 1.0))
        base_ref[:, cut] += jnp.where(top, averaged, d)

    land(traces2)
    acc = jnp.zeros((128, LANES), F32)
    for k, (_, _, present) in enumerate(slots):
        half = (0.5 * present.astype(F32)) * part2_ref[k]
        term_ref[0:4, :] = half
        term_ref[4:8, :] = half
        acc = acc + scatter_dot(term_ref[...], paired(hi_ref[k : k + 1, :]), 2, 8, hot_ref[k])
    sums = acc[:64] + acc[64:]
    low = low_half()
    for a in range(PA):
        tile = sums[8 * a : 8 * a + 8]
        add_row(base_ref, a * PLANE, jnp.where(low, 0.0, pltpu.roll(tile, 4, 0)))
        add_row(base_ref, a * PLANE + 9 * PC, jnp.where(low, 0.0, tile))
    add_extra(base_ref, jnp.where(low, 0.0, pltpu.roll(sums[48:56], 4, 0)))
    for copies in (rims, traces, rims2, traces2):
        drain(copies)


def finish_kernel(base_ref, res_ref, new_ref):
    for c in range(3):
        new_ref[c] = base_ref[c : c + 1, :CP]
    for c in range(4):
        res_ref[c] = base_ref[4 + c : 5 + c, :CP]


VMEM = pl.BlockSpec(memory_space=pltpu.VMEM)
SMEM = pl.BlockSpec(memory_space=pltpu.SMEM)
HBM = pl.BlockSpec(memory_space=pltpu.HBM)


def shaped(*shape):
    return jax.ShapeDtypeStruct(shape, F32)


def shards(state, mesh_vel, disp, elem_size, live_slabs, trace_rows, penalty):
    base = pl.pallas_call(
        main_kernel,
        out_shape=shaped(8, WIDE),
        in_specs=[SMEM] + [HBM] * 6,
        out_specs=VMEM,
        scratch_shapes=[
            pltpu.VMEM((4, 1, CP), F32),
            pltpu.VMEM((3, 1, CP), F32),
            pltpu.VMEM((3, 1, CP), F32),
            pltpu.VMEM((1, SLABS * SLOTS), F32),
            pltpu.VMEM((4, SLOTS), jnp.int32),
            pltpu.VMEM((4, SLOTS), F32),
            pltpu.VMEM((8, WIDE), F32),
            pltpu.VMEM((8, WIDE), F32),
            pltpu.VMEM((6, 8 * ROWS, LANES), F32),
            pltpu.VMEM((PA, 9, 15, 8, LANES), F32),
            pltpu.VMEM((PA, 9, 12, 8, LANES), F32),
            pltpu.VMEM((SLABS, 8, LANES), F32),
            pltpu.VMEM((8 * TABS, LANES), F32),
            pltpu.VMEM((8, RIM + LANES), F32),
            pltpu.VMEM((4, 8, SLOTS), F32),
            pltpu.VMEM((4, 8, SLOTS), F32),
            pltpu.VMEM((4, 4, SLOTS), F32),
            pltpu.VMEM((4, 4, SLOTS), F32),
            pltpu.VMEM((2, 4, RIM), F32),
            pltpu.VMEM((2, 4, RIM), F32),
            pltpu.VMEM((2, 4, RIM), F32),
            pltpu.VMEM((2, 4, RIM), F32),
            pltpu.VMEM((4, LANES, SLOTS), BF16),
            pltpu.VMEM((4, SLOTS), jnp.int32),
            pltpu.VMEM((8, WIDE), F32),
            pltpu.VMEM((8, SLOTS), F32),
            pltpu.SemaphoreType.DMA((13,)),
            pltpu.SemaphoreType.DMA((12,)),
            pltpu.SemaphoreType.DMA((12,)),
        ],
        compiler_params=pltpu.CompilerParams(
            vmem_limit_bytes=48 << 20, collective_id=0, has_side_effects=True
        ),
    )(live_slabs, *[pltpu.with_memory_space_constraint(x, pltpu.HBM) for x in (state, mesh_vel, disp, elem_size, trace_rows, penalty)])
    return pl.pallas_call(
        finish_kernel,
        out_shape=(shaped(4, 1, CP), shaped(3, 1, CP)),
        in_specs=[VMEM],
        out_specs=(VMEM, VMEM),
        compiler_params=pltpu.CompilerParams(vmem_limit_bytes=16 << 20),
    )(base)


def solution(mesh):
    return jax.shard_map(
        shards,
        mesh=mesh,
        in_specs=(
            P(None, "group", "dom"),
            P(None, "group", "dom"),
            P(None, "group", "dom"),
            P("group", "dom"),
            P("group", "dom"),
            P("group", "dom", None, None),
            P("group", "dom", None, None),
        ),
        out_specs=(P(None, "group", "dom"), P(None, "group", "dom")),
        check_vma=False,
    )
```

```python
import math

import jax
import jax.numpy as jnp
from jax import lax
from jax.experimental import pallas as pl
from jax.experimental.pallas import tpu as pltpu
from jax.sharding import PartitionSpec as P

PA = 6
PB = 10
PC = 130
CP = PA * PB * PC
SLABS = 4
ROWS = PA * PB
PLANE = PB * PC
LANES = 128
COLS = 61
WIDE = (COLS + 1) * LANES
SLOTS = 1024
SHARED = 2 * PLANE
RIM = 21 * LANES
LAST_COL = 4 * PLANE // LANES
LAST_OFF = 4 * PLANE % LANES
TABS = 14

DT = 0.5
NU = 0.05
S = math.sqrt(0.15)
W_EDGE = 5.0 / 18.0
W_MID = 8.0 / 18.0
F32 = jnp.float32
BF16 = jnp.bfloat16


def face_extras():
    out = []
    for a in range(PA):
        base = a * PLANE
        out += [base + b * PC + 129 for b in range(PB)]
        out += [base + 128, base + 9 * PC + 128]
        out += [base + b * PC for b in range(1, PB - 1)]
    return out


EXTRAS = face_extras()


def lane_iota():
    return lax.broadcasted_iota(jnp.int32, (8, LANES), 1)


def take_row(ref, start):
    off = start % LANES
    col = start - off
    first = ref[:, col : col + LANES]
    if off == 0:
        return first
    second = ref[:, col + LANES : col + 2 * LANES]
    mixed = jnp.where(lane_iota() >= off, first, second)
    return pltpu.roll(mixed, LANES - off, 1)


def add_row(ref, start, val):
    off = start % LANES
    col = start - off
    if off == 0:
        ref[:, col : col + LANES] += val
        return
    turned = pltpu.roll(val, off, 1)
    lane = lane_iota()
    ref[:, col : col + LANES] += jnp.where(lane >= off, turned, 0.0)
    ref[:, col + LANES : col + 2 * LANES] += jnp.where(lane < off, turned, 0.0)


def locate(row):
    plane = jnp.zeros_like(row)
    for k in range(1, PA):
        plane = plane + (row >= k * PLANE).astype(jnp.int32)
    rest = row - plane * PLANE
    along_b = jnp.zeros_like(row)
    for k in range(1, PB):
        along_b = along_b + (rest >= k * PC).astype(jnp.int32)
    along_c = rest - along_b * PC
    top = along_b == PB - 1
    straight = ((along_b == 0) | top) & (along_c < LANES)
    which = jnp.where(
        along_c == 129,
        along_b,
        jnp.where(along_c == 128, jnp.where(top, 11, 10), 11 + along_b),
    )
    hi = jnp.where(straight, 2 * plane + top.astype(jnp.int32), 12)
    lo = jnp.where(straight, along_c, 20 * plane + which)
    return hi, lo


def one_hot(lo):
    return (lax.broadcasted_iota(jnp.int32, (LANES, SLOTS), 0) == lo).astype(F32).astype(BF16)


def split_bf16(val):
    high = val.astype(BF16)
    low = (val - high.astype(F32)).astype(BF16)
    return high, low


def face_extra(x_ref):
    lane = lane_iota()
    extra = jnp.zeros((8, LANES), F32)
    for k, flat in enumerate(EXTRAS):
        extra = jnp.where(lane == k, x_ref[:, flat : flat + 1], extra)
    return extra


def face_tables(x_ref, tab_ref):
    for a in range(PA):
        tab_ref[16 * a : 16 * a + 8, :] = take_row(x_ref, a * PLANE)
        tab_ref[16 * a + 8 : 16 * a + 16, :] = take_row(x_ref, a * PLANE + 9 * PC)
    tab_ref[96:104, :] = face_extra(x_ref)
    tab_ref[104:112, :] = jnp.zeros((8, LANES), F32)
    high, low = split_bf16(tab_ref[...])
    return jnp.concatenate([high, low], axis=0)


def gather_slots(table, hi, hot):
    full = jnp.dot(table, hot, preferred_element_type=F32)
    out = jnp.zeros((8, SLOTS), F32)
    for h in range(13):
        piece = full[8 * h : 8 * h + 8] + full[112 + 8 * h : 120 + 8 * h]
        out = jnp.where(hi == h, piece, out)
    return out


def low_half():
    return lax.broadcasted_iota(jnp.int32, (8, LANES), 0) < 4


def pair_tables(x_ref):
    low = low_half()
    tiles = []
    for a in range(PA):
        front = pltpu.roll(take_row(x_ref, a * PLANE), 4, 0)
        tiles.append(jnp.where(low, front, take_row(x_ref, a * PLANE + 9 * PC)))
    tiles.append(jnp.where(low, pltpu.roll(face_extra(x_ref), 4, 0), 0.0))
    tiles.append(jnp.zeros((8, LANES), F32))
    high, low = split_bf16(jnp.concatenate(tiles, axis=0))
    return jnp.concatenate([high, low], axis=0)


def paired(hi):
    return hi - (lax.broadcasted_iota(jnp.int32, (8, SLOTS), 0) >= 4).astype(jnp.int32)


def gather_pairs(table, hi, hot):
    full = jnp.dot(table, hot, preferred_element_type=F32)
    which = paired(hi)
    out = jnp.zeros((8, SLOTS), F32)
    for p in range(7):
        piece = full[8 * p : 8 * p + 8] + full[64 + 8 * p : 72 + 8 * p]
        out = jnp.where(which == 2 * p, piece, out)
    return out[0:4] + out[4:8]


def scatter_dot(term, which, step, tiles, hot):
    high = term.astype(BF16).astype(F32)
    low = term - high
    spread = [jnp.where(which == step * p, high, 0.0) for p in range(tiles)]
    spread += [jnp.where(which == step * p, low, 0.0) for p in range(tiles)]
    lhs = jnp.concatenate(spread, axis=0).astype(BF16)
    return lax.dot_general(lhs, hot, (((1,), (1,)), ((), ())), preferred_element_type=F32)


def add_extra(d_ref, extra):
    lane = lane_iota()
    by_col = {}
    for k, flat in enumerate(EXTRAS):
        by_col.setdefault(flat // LANES, []).append((k, flat % LANES))
    for col, entries in by_col.items():
        val = d_ref[:, col * LANES : (col + 1) * LANES]
        for k, at in entries:
            val = val + jnp.where(lane == at, extra[:, k : k + 1], 0.0)
        d_ref[:, col * LANES : (col + 1) * LANES] = val


def fwd_value(x0, x1, x2):
    even, odd = x0 + x2, x2 - x0
    base = 0.2 * even + 0.6 * x1
    mid = 0.125 * even + 0.75 * x1
    side = (S / 2) * odd
    return (base - side, mid, base + side)


def fwd_slope(x0, x1, x2):
    half = 0.5 * (x2 - x0)
    bend = S * ((x0 + x2) - 2.0 * x1)
    return (half - bend, half, half + bend)


def back_value(y0, y1, y2):
    even, odd = y0 + y2, y2 - y0
    ends = (W_EDGE * 0.2) * even + (W_MID * 0.125) * y1
    side = (W_EDGE * S / 2) * odd
    return (ends - side, (W_EDGE * 0.6) * even + (W_MID * 0.75) * y1, ends + side)


def back_slope(z0, z1, z2):
    turn = (W_EDGE * S) * (z2 - z0)
    half = (0.5 * W_EDGE) * (z0 + z2) + (0.5 * W_MID) * z1
    return (turn - half, -2.0 * turn, turn + half)


def both(value, slope):
    return tuple(v + d for v, d in zip(back_value(*value), back_slope(*slope)))


def strided(start):
    return pl.ds(start, 8, stride=8)


def element_stage(live, x_ref, q_ref, g_ref, acc_ref, h_ref, out_ref):
    for r in range(ROWS):
        taps = [take_row(x_ref, r * PC + s) for s in range(3)]
        for k, val in enumerate(fwd_value(*taps) + fwd_slope(*taps)):
            q_ref[k, 8 * r : 8 * r + 8, :] = val

    def along_b(a, carry):
        for f in range(7):
            for qc in range(3):
                value = [q_ref[qc, strided(a * 80 + 8 * s + f), :] for s in range(3)]
                if f >= 4:
                    for qb, val in enumerate(fwd_value(*value)):
                        g_ref[a, 3 * qb + qc, 8 + f] = val
                    continue
                slope = [q_ref[3 + qc, strided(a * 80 + 8 * s + f), :] for s in range(3)]
                vv = fwd_value(*value)
                dv = fwd_slope(*value)
                vd = fwd_value(*slope)
                for qb in range(3):
                    g_ref[a, 3 * qb + qc, 3 * f] = vv[qb]
                    g_ref[a, 3 * qb + qc, 3 * f + 1] = dv[qb]
                    g_ref[a, 3 * qb + qc, 3 * f + 2] = vd[qb]
        return carry

    lax.fori_loop(0, PA, along_b, 0)

    zero = jnp.zeros((8, LANES), F32)

    def clear(a, carry):
        for q in range(9):
            for k in range(12):
                acc_ref[a, q, k] = zero
        return carry

    lax.fori_loop(0, 2, clear, 0)

    def points(slab, q):
        h = h_ref[slab]
        outer = jnp.where(live > slab, h, 0.0)

        def taps(slot):
            return [g_ref[slab + s, q, slot] for s in range(3)]

        grads = [
            [fwd_slope(*taps(3 * f)), fwd_value(*taps(3 * f + 1)), fwd_value(*taps(3 * f + 2))]
            for f in range(4)
        ]
        pressure = fwd_value(*taps(9))
        adv = [fwd_value(*taps(12 + c)) for c in range(3)]
        inv = 1.0 / h
        inv2 = inv * inv
        four = 4.0 * inv2
        fixed = 4.0 / DT**2 + (36.0 * NU**2) * (inv2 * inv2)
        h2 = (h * h) * (1.0 / 12.0)
        coef_f = [[None] * 3 for _ in range(4)]
        coef_k = [[[None] * 3 for _ in range(4)] for _ in range(3)]
        for t in range(3):
            a = [adv[c][t] for c in range(3)]
            conv = [
                a[0] * grads[c][0][t] + a[1] * grads[c][1][t] + a[2] * grads[c][2][t]
                for c in range(3)
            ]
            mom = [conv[c] + grads[3][c][t] for c in range(3)]
            cont = grads[0][0][t] + grads[1][1][t] + grads[2][2][t]
            total = fixed + four * (a[0] * a[0] + a[1] * a[1] + a[2] * a[2])
            tau = lax.rsqrt(total)
            press = h * pressure[t] - h2 * (total * tau) * cont
            scaled = [tau * mom[c] for c in range(3)]
            for c in range(3):
                coef_f[c][t] = h * conv[c]
                coef_k[c][3][t] = scaled[c]
                for d in range(3):
                    val = NU * grads[c][d][t] + a[d] * scaled[c]
                    coef_k[d][c][t] = val - press if d == c else val
            coef_f[3][t] = h * cont
        for c in range(4):
            parts = (
                both(coef_f[c], coef_k[0][c]),
                back_value(*coef_k[1][c]),
                back_value(*coef_k[2][c]),
            )
            for k, part in enumerate(parts):
                for s in range(2):
                    acc_ref[slab + s, q, 3 * c + k] += outer * part[s]
                acc_ref[slab + 2, q, 3 * c + k] = outer * part[2]

    def slab_loop(slab, carry):
        def point_loop(i, inner):
            for k in range(3):
                points(slab, 3 * i + k)
            return inner

        return lax.fori_loop(0, 3, point_loop, carry)

    lax.fori_loop(0, SLABS, slab_loop, 0)

    for a in range(PA):
        for k in range(6):
            q_ref[k, a * 80 + 64 : a * 80 + 72, :] = zero
            q_ref[k, a * 80 + 72 : a * 80 + 80, :] = zero

    def back_b(a, carry):
        for c in range(4):
            for qc in range(3):
                pieces = [
                    [acc_ref[a, 3 * qb + qc, 3 * c + k] for qb in range(3)] for k in range(3)
                ]
                straight = both(pieces[0], pieces[1])
                sloped = back_value(*pieces[2])
                at = strided(a * 80 + 4 + c)
                q_ref[qc, at, :] = straight[0]
                q_ref[3 + qc, at, :] = sloped[0]
                for s in range(1, 3):
                    at = strided(a * 80 + 8 * s + 4 + c)
                    q_ref[qc, at, :] += straight[s]
                    q_ref[3 + qc, at, :] += sloped[s]
        return carry

    lax.fori_loop(0, PA, back_b, 0)

    lane = lane_iota()
    pending = zero
    for r in range(ROWS):
        y = [q_ref[k, 8 * r : 8 * r + 8, :] for k in range(6)]
        y0, y1, y2 = both(y[:3], y[3:])
        y1 = pltpu.roll(y1, 1, 1)
        y2 = pltpu.roll(y2, 2, 1)
        main = y0 + jnp.where(lane >= 1, y1, 0.0) + jnp.where(lane >= 2, y2, 0.0)
        tail = jnp.where(lane < 1, y1, 0.0) + jnp.where(lane < 2, y2, 0.0)
        off = 2 * r
        if off:
            main = pltpu.roll(main, off, 1)
            tail = pltpu.roll(tail, off, 1)
        out_ref[:, r * LANES : (r + 1) * LANES] = jnp.where(lane >= off, main, pending)
        pending = jnp.where(lane < off, main, tail)
    out_ref[:, ROWS * LANES : (ROWS + 1) * LANES] = pending
    out_ref[:, COLS * LANES :] = zero


def rim_cut(col):
    return lane_iota() < min(LANES, SHARED - col * LANES)


def widen(rim_ref, wide_ref, low):
    wide_ref[...] = jnp.zeros_like(wide_ref)
    wide_ref[low : low + 4, :RIM] = rim_ref[...]


def cut_rims(x_ref, low, rim_ref):
    rim_ref[0] = x_ref[low : low + 4, :RIM]
    rim_ref[1] = x_ref[low : low + 4, LAST_COL * LANES : LAST_COL * LANES + RIM]


def main_kernel(
    live_ref, state_hbm, mesh_hbm, disp_hbm, size_hbm, rows_hbm, pen_hbm,
    base_ref,
    state_ref, mesh_ref, disp_ref, size_ref, rows_ref, pen_ref, x_ref, f_ref, q_ref, g_ref, acc_ref, h_ref, tab_ref, wide_ref,
    own_ref, part_ref, own2_ref, part2_ref, rim_ref, rim_in_ref, rim2_ref, rim2_in_ref,
    hot_ref, hi_ref, d_ref, term_ref, load_sem, send_sem, recv_sem,
):
    groups = lax.axis_size("group")
    doms = lax.axis_size("dom")
    group = lax.axis_index("group")
    dom = lax.axis_index("dom")
    stride = groups // 2
    offsets = (1, -1, stride, -stride)
    slots = [
        (group + step, dom, (group + step >= 0) & (group + step < groups)) for step in offsets
    ]
    sides = [(group, dom - 1, dom > 0), (group, dom + 1, dom < doms - 1)]
    loads = []
    for src, dst, count in ((state_hbm, state_ref, 4), (mesh_hbm, mesh_ref, 3), (disp_hbm, disp_ref, 3)):
        for c in range(count):
            loads.append(
                pltpu.make_async_copy(src.at[c], dst.at[c], load_sem.at[len(loads)])
            )
    small = (
        (size_hbm, size_ref),
        (rows_hbm.at[0, 0], rows_ref),
        (pen_hbm.at[0, 0], pen_ref),
    )
    for src, dst in small:
        loads.append(pltpu.make_async_copy(src, dst, load_sem.at[len(loads)]))
    for load in loads:
        load.start()

    barrier = pltpu.get_barrier_semaphore()
    peers = 0
    for to_group, to_dom, present in slots + sides:
        peers = peers + present.astype(jnp.int32)

        @pl.when(present)
        def _():
            pl.semaphore_signal(
                barrier, inc=1, device_id=(to_group, to_dom), device_id_type=pl.DeviceIdType.MESH
            )

    def remote(src, dst, at, to, arrive):
        return pltpu.make_async_remote_copy(
            src_ref=src,
            dst_ref=dst,
            send_sem=send_sem.at[at],
            recv_sem=recv_sem.at[arrive],
            device_id=(to[0], to[1]),
            device_id_type=pl.DeviceIdType.MESH,
        )

    def exchange(out_ref, in_ref, peers_of, sem):
        return [
            (to[2], remote(out_ref.at[k], in_ref.at[k ^ 1], sem + k, to, sem + (k ^ 1)),
             remote(out_ref.at[k], in_ref.at[k], sem + k, to, sem + k))
            for k, to in enumerate(peers_of)
        ]

    def launch(copies):
        for present, out, _ in copies:

            @pl.when(present)
            def _():
                out.start()

    def land(copies):
        for present, _, back in copies:

            @pl.when(present)
            def _():
                back.wait_recv()

    def drain(copies):
        for present, out, _ in copies:

            @pl.when(present)
            def _():
                out.wait_send()

    traces = exchange(own_ref, part_ref, slots, 0)
    traces2 = exchange(own2_ref, part2_ref, slots, 4)
    rims = exchange(rim_ref, rim_in_ref, sides, 8)
    rims2 = exchange(rim2_ref, rim2_in_ref, sides, 10)

    for load in loads[:7] + loads[10:11]:
        load.wait()
    for c in range(3):
        f_ref[4 + c : 5 + c, :CP] = state_ref[c] - mesh_ref[c]
    f_ref[7:8, :CP] = jnp.zeros((1, CP), F32)
    for c in range(4):
        f_ref[c : c + 1, :CP] = state_ref[c]
    f_ref[:, COLS * LANES :] = jnp.zeros((8, LANES), F32)
    for k in range(32):
        h_ref[k // 8, k % 8 : k % 8 + 1, :] = size_ref[:, k * LANES : (k + 1) * LANES]
    live = jnp.zeros((8, LANES), jnp.int32) + live_ref[0, 0]
    element_stage(live, f_ref, q_ref, g_ref, acc_ref, h_ref, base_ref)
    cut_rims(base_ref, 4, rim2_ref)
    pl.semaphore_wait(barrier, peers)
    launch(rims2)

    for load in loads[7:10] + loads[11:]:
        load.wait()
    for c in range(3):
        x_ref[c : c + 1, :CP] = disp_ref[c] + 0.5 * mesh_ref[c]
    x_ref[3:4, :CP] = jnp.zeros((1, CP), F32)
    for c in range(4):
        x_ref[4 + c : 5 + c, :CP] = state_ref[c]
    x_ref[:, COLS * LANES :] = jnp.zeros((8, LANES), F32)
    cut_rims(x_ref, 0, rim_ref)
    launch(rims)
    table = face_tables(x_ref, tab_ref)
    for k in range(4):
        hi, lo = locate(rows_ref[k : k + 1, :])
        hi_ref[k : k + 1, :] = hi
        hot = one_hot(lo)
        hot_ref[k] = hot
        own_ref[k] = gather_slots(table, hi, hot)
    launch(traces)

    for k, (_, _, present) in enumerate(slots):

        @pl.when(jnp.logical_not(present))
        def _():
            part_ref[k] = jnp.zeros((8, SLOTS), F32)
            part2_ref[k] = jnp.zeros((4, SLOTS), F32)

    for k, (_, _, present) in enumerate(sides):

        @pl.when(jnp.logical_not(present))
        def _():
            rim_in_ref[k] = jnp.zeros((4, RIM), F32)
            rim2_in_ref[k] = jnp.zeros((4, RIM), F32)

    land(rims2)
    widen(rim2_in_ref.at[0], wide_ref, 4)
    for col in range(21):
        val = jnp.where(rim_cut(col), take_row(wide_ref, LAST_OFF + col * LANES), 0.0)
        base_ref[:, col * LANES : (col + 1) * LANES] += val
    widen(rim2_in_ref.at[1], wide_ref, 4)
    for col in range(21):
        val = jnp.where(rim_cut(col), wide_ref[:, col * LANES : (col + 1) * LANES], 0.0)
        add_row(base_ref, LAST_COL * LANES + LAST_OFF + col * LANES, val)
    table = pair_tables(base_ref)
    for k in range(4):
        own2_ref[k] = gather_pairs(table, hi_ref[k : k + 1, :], hot_ref[k])
    launch(traces2)

    d_ref[...] = jnp.zeros_like(d_ref)
    top = lax.broadcasted_iota(jnp.int32, (8, LANES), 0) < 3
    for col in range(COLS):
        cut = slice(col * LANES, (col + 1) * LANES)
        base_ref[:, cut] = jnp.where(top, x_ref[:, cut], base_ref[:, cut])
    land(rims)
    has_prev = 0.5 * sides[0][2].astype(F32)
    has_next = 0.5 * sides[1][2].astype(F32)
    widen(rim_in_ref.at[0], wide_ref, 0)
    for col in range(21):
        cut = slice(col * LANES, (col + 1) * LANES)
        val = take_row(wide_ref, LAST_OFF + col * LANES) - x_ref[:, cut]
        base_ref[:, cut] += jnp.where(rim_cut(col) & top, has_prev * val, 0.0)
    widen(rim_in_ref.at[1], wide_ref, 0)
    for col in range(21):
        start = LAST_COL * LANES + LAST_OFF + col * LANES
        val = wide_ref[:, col * LANES : (col + 1) * LANES] - take_row(x_ref, start)
        add_row(base_ref, start, jnp.where(rim_cut(col) & top, has_next * val, 0.0))
    land(traces)
    acc = jnp.zeros((2 * 8 * TABS, LANES), F32)
    for k, (_, _, present) in enumerate(slots):
        live_slot = present.astype(F32)
        gap = (part_ref[k] - own_ref[k]) * live_slot
        term_ref[...] = gap
        term_ref[3:4, :] = jnp.zeros((1, SLOTS), F32) + live_slot
        term_ref[4:8, :] = -pen_ref[k : k + 1, :] * gap[4:8] - (0.5 * live_slot) * own2_ref[k]
        acc = acc + scatter_dot(term_ref[...], hi_ref[k : k + 1, :], 1, TABS, hot_ref[k])
    sums = acc[: 8 * TABS] + acc[8 * TABS :]
    for a in range(PA):
        add_row(d_ref, a * PLANE, sums[16 * a : 16 * a + 8])
        add_row(d_ref, a * PLANE + 9 * PC, sums[16 * a + 8 : 16 * a + 16])
    add_extra(d_ref, sums[96:104])
    for col in range(COLS):
        cut = slice(col * LANES, (col + 1) * LANES)
        d = d_ref[:, cut]
        averaged = d / (2.0 * jnp.maximum(d[3:4], 1.0))
        base_ref[:, cut] += jnp.where(top, averaged, d)

    land(traces2)
    acc = jnp.zeros((128, LANES), F32)
    for k, (_, _, present) in enumerate(slots):
        half = (0.5 * present.astype(F32)) * part2_ref[k]
        term_ref[0:4, :] = half
        term_ref[4:8, :] = half
        acc = acc + scatter_dot(term_ref[...], paired(hi_ref[k : k + 1, :]), 2, 8, hot_ref[k])
    sums = acc[:64] + acc[64:]
    low = low_half()
    for a in range(PA):
        tile = sums[8 * a : 8 * a + 8]
        add_row(base_ref, a * PLANE, jnp.where(low, 0.0, pltpu.roll(tile, 4, 0)))
        add_row(base_ref, a * PLANE + 9 * PC, jnp.where(low, 0.0, tile))
    add_extra(base_ref, jnp.where(low, 0.0, pltpu.roll(sums[48:56], 4, 0)))
    for copies in (rims, traces, rims2, traces2):
        drain(copies)


def finish_kernel(base_ref, res_ref, new_ref):
    for c in range(3):
        new_ref[c] = base_ref[c : c + 1, :CP]
    for c in range(4):
        res_ref[c] = base_ref[4 + c : 5 + c, :CP]


VMEM = pl.BlockSpec(memory_space=pltpu.VMEM)
SMEM = pl.BlockSpec(memory_space=pltpu.SMEM)
HBM = pl.BlockSpec(memory_space=pltpu.HBM)


def shaped(*shape):
    return jax.ShapeDtypeStruct(shape, F32)


def shards(state, mesh_vel, disp, elem_size, live_slabs, trace_rows, penalty):
    base = pl.pallas_call(
        main_kernel,
        out_shape=shaped(8, WIDE),
        in_specs=[SMEM] + [HBM] * 6,
        out_specs=VMEM,
        scratch_shapes=[
            pltpu.VMEM((4, 1, CP), F32),
            pltpu.VMEM((3, 1, CP), F32),
            pltpu.VMEM((3, 1, CP), F32),
            pltpu.VMEM((1, SLABS * SLOTS), F32),
            pltpu.VMEM((4, SLOTS), jnp.int32),
            pltpu.VMEM((4, SLOTS), F32),
            pltpu.VMEM((8, WIDE), F32),
            pltpu.VMEM((8, WIDE), F32),
            pltpu.VMEM((6, 8 * ROWS, LANES), F32),
            pltpu.VMEM((PA, 9, 15, 8, LANES), F32),
            pltpu.VMEM((PA, 9, 12, 8, LANES), F32),
            pltpu.VMEM((SLABS, 8, LANES), F32),
            pltpu.VMEM((8 * TABS, LANES), F32),
            pltpu.VMEM((8, RIM + LANES), F32),
            pltpu.VMEM((4, 8, SLOTS), F32),
            pltpu.VMEM((4, 8, SLOTS), F32),
            pltpu.VMEM((4, 4, SLOTS), F32),
            pltpu.VMEM((4, 4, SLOTS), F32),
            pltpu.VMEM((2, 4, RIM), F32),
            pltpu.VMEM((2, 4, RIM), F32),
            pltpu.VMEM((2, 4, RIM), F32),
            pltpu.VMEM((2, 4, RIM), F32),
            pltpu.VMEM((4, LANES, SLOTS), BF16),
            pltpu.VMEM((4, SLOTS), jnp.int32),
            pltpu.VMEM((8, WIDE), F32),
            pltpu.VMEM((8, SLOTS), F32),
            pltpu.SemaphoreType.DMA((13,)),
            pltpu.SemaphoreType.DMA((12,)),
            pltpu.SemaphoreType.DMA((12,)),
        ],
        compiler_params=pltpu.CompilerParams(
            vmem_limit_bytes=48 << 20, collective_id=0, has_side_effects=True
        ),
    )(live_slabs, *[pltpu.with_memory_space_constraint(x, pltpu.HBM) for x in (state, mesh_vel, disp, elem_size, trace_rows, penalty)])
    return pl.pallas_call(
        finish_kernel,
        out_shape=(shaped(4, 1, CP), shaped(3, 1, CP)),
        in_specs=[VMEM],
        out_specs=(VMEM, VMEM),
        compiler_params=pltpu.CompilerParams(vmem_limit_bytes=16 << 20),
    )(base)


def solution(mesh):
    return jax.shard_map(
        shards,
        mesh=mesh,
        in_specs=(
            P(None, "group", "dom"),
            P(None, "group", "dom"),
            P(None, "group", "dom"),
            P("group", "dom"),
            P("group", "dom"),
            P("group", "dom", None, None),
            P("group", "dom", None, None),
        ),
        out_specs=(P(None, "group", "dom"), P(None, "group", "dom")),
        check_vma=False,
    )
```

```python
import math

import jax
import jax.numpy as jnp
from jax import lax
from jax.experimental import pallas as pl
from jax.experimental.pallas import tpu as pltpu
from jax.sharding import PartitionSpec as P

PA = 6
PB = 10
PC = 130
CP = PA * PB * PC
SLABS = 4
ROWS = PA * PB
PLANE = PB * PC
LANES = 128
COLS = 61
WIDE = (COLS + 1) * LANES
SLOTS = 1024
SHARED = 2 * PLANE
RIM = 21 * LANES
LAST_COL = 4 * PLANE // LANES
LAST_OFF = 4 * PLANE % LANES
TABS = 14

DT = 0.5
NU = 0.05
S = math.sqrt(0.15)
W_EDGE = 5.0 / 18.0
W_MID = 8.0 / 18.0
F32 = jnp.float32
BF16 = jnp.bfloat16


def face_extras():
    out = []
    for a in range(PA):
        base = a * PLANE
        out += [base + b * PC + 129 for b in range(PB)]
        out += [base + 128, base + 9 * PC + 128]
        out += [base + b * PC for b in range(1, PB - 1)]
    return out


EXTRAS = face_extras()


def lane_iota():
    return lax.broadcasted_iota(jnp.int32, (8, LANES), 1)


def take_row(ref, start):
    off = start % LANES
    col = start - off
    first = ref[:, col : col + LANES]
    if off == 0:
        return first
    second = ref[:, col + LANES : col + 2 * LANES]
    mixed = jnp.where(lane_iota() >= off, first, second)
    return pltpu.roll(mixed, LANES - off, 1)


def add_row(ref, start, val):
    off = start % LANES
    col = start - off
    if off == 0:
        ref[:, col : col + LANES] += val
        return
    turned = pltpu.roll(val, off, 1)
    lane = lane_iota()
    ref[:, col : col + LANES] += jnp.where(lane >= off, turned, 0.0)
    ref[:, col + LANES : col + 2 * LANES] += jnp.where(lane < off, turned, 0.0)


def locate(row):
    plane = jnp.zeros_like(row)
    for k in range(1, PA):
        plane = plane + (row >= k * PLANE).astype(jnp.int32)
    rest = row - plane * PLANE
    along_b = jnp.zeros_like(row)
    for k in range(1, PB):
        along_b = along_b + (rest >= k * PC).astype(jnp.int32)
    along_c = rest - along_b * PC
    top = along_b == PB - 1
    straight = ((along_b == 0) | top) & (along_c < LANES)
    which = jnp.where(
        along_c == 129,
        along_b,
        jnp.where(along_c == 128, jnp.where(top, 11, 10), 11 + along_b),
    )
    hi = jnp.where(straight, 2 * plane + top.astype(jnp.int32), 12)
    lo = jnp.where(straight, along_c, 20 * plane + which)
    return hi, lo


def one_hot(lo):
    return (lax.broadcasted_iota(jnp.int32, (LANES, SLOTS), 0) == lo).astype(F32).astype(BF16)


def split_bf16(val):
    high = val.astype(BF16)
    low = (val - high.astype(F32)).astype(BF16)
    return high, low


def face_extra(x_ref):
    lane = lane_iota()
    extra = jnp.zeros((8, LANES), F32)
    for k, flat in enumerate(EXTRAS):
        extra = jnp.where(lane == k, x_ref[:, flat : flat + 1], extra)
    return extra


def face_tables(x_ref, tab_ref):
    for a in range(PA):
        tab_ref[16 * a : 16 * a + 8, :] = take_row(x_ref, a * PLANE)
        tab_ref[16 * a + 8 : 16 * a + 16, :] = take_row(x_ref, a * PLANE + 9 * PC)
    tab_ref[96:104, :] = face_extra(x_ref)
    tab_ref[104:112, :] = jnp.zeros((8, LANES), F32)
    high, low = split_bf16(tab_ref[...])
    return jnp.concatenate([high, low], axis=0)


def gather_slots(table, hi, hot):
    full = jnp.dot(table, hot, preferred_element_type=F32)
    out = jnp.zeros((8, SLOTS), F32)
    for h in range(13):
        piece = full[8 * h : 8 * h + 8] + full[112 + 8 * h : 120 + 8 * h]
        out = jnp.where(hi == h, piece, out)
    return out


def low_half():
    return lax.broadcasted_iota(jnp.int32, (8, LANES), 0) < 4


def pair_tables(x_ref):
    low = low_half()
    tiles = []
    for a in range(PA):
        front = pltpu.roll(take_row(x_ref, a * PLANE), 4, 0)
        tiles.append(jnp.where(low, front, take_row(x_ref, a * PLANE + 9 * PC)))
    tiles.append(jnp.where(low, pltpu.roll(face_extra(x_ref), 4, 0), 0.0))
    tiles.append(jnp.zeros((8, LANES), F32))
    high, low = split_bf16(jnp.concatenate(tiles, axis=0))
    return jnp.concatenate([high, low], axis=0)


def paired(hi):
    return hi - (lax.broadcasted_iota(jnp.int32, (8, SLOTS), 0) >= 4).astype(jnp.int32)


def gather_pairs(table, hi, hot):
    full = jnp.dot(table, hot, preferred_element_type=F32)
    which = paired(hi)
    out = jnp.zeros((8, SLOTS), F32)
    for p in range(7):
        piece = full[8 * p : 8 * p + 8] + full[64 + 8 * p : 72 + 8 * p]
        out = jnp.where(which == 2 * p, piece, out)
    return out[0:4] + out[4:8]


def scatter_dot(term, which, step, tiles, hot):
    high = term.astype(BF16).astype(F32)
    low = term - high
    spread = [jnp.where(which == step * p, high, 0.0) for p in range(tiles)]
    spread += [jnp.where(which == step * p, low, 0.0) for p in range(tiles)]
    lhs = jnp.concatenate(spread, axis=0).astype(BF16)
    return lax.dot_general(lhs, hot, (((1,), (1,)), ((), ())), preferred_element_type=F32)


def add_extra(d_ref, extra):
    lane = lane_iota()
    by_col = {}
    for k, flat in enumerate(EXTRAS):
        by_col.setdefault(flat // LANES, []).append((k, flat % LANES))
    for col, entries in by_col.items():
        val = d_ref[:, col * LANES : (col + 1) * LANES]
        for k, at in entries:
            val = val + jnp.where(lane == at, extra[:, k : k + 1], 0.0)
        d_ref[:, col * LANES : (col + 1) * LANES] = val


def fwd_value(x0, x1, x2):
    even, odd = x0 + x2, x2 - x0
    base = 0.2 * even + 0.6 * x1
    mid = 0.125 * even + 0.75 * x1
    side = (S / 2) * odd
    return (base - side, mid, base + side)


def fwd_slope(x0, x1, x2):
    half = 0.5 * (x2 - x0)
    bend = S * ((x0 + x2) - 2.0 * x1)
    return (half - bend, half, half + bend)


def back_value(y0, y1, y2):
    even, odd = y0 + y2, y2 - y0
    ends = (W_EDGE * 0.2) * even + (W_MID * 0.125) * y1
    side = (W_EDGE * S / 2) * odd
    return (ends - side, (W_EDGE * 0.6) * even + (W_MID * 0.75) * y1, ends + side)


def back_slope(z0, z1, z2):
    turn = (W_EDGE * S) * (z2 - z0)
    half = (0.5 * W_EDGE) * (z0 + z2) + (0.5 * W_MID) * z1
    return (turn - half, -2.0 * turn, turn + half)


def both(value, slope):
    return tuple(v + d for v, d in zip(back_value(*value), back_slope(*slope)))


def strided(start):
    return pl.ds(start, 8, stride=8)


def element_stage(live, x_ref, q_ref, g_ref, acc_ref, h_ref, out_ref):
    for r in range(ROWS):
        taps = [take_row(x_ref, r * PC + s) for s in range(3)]
        for k, val in enumerate(fwd_value(*taps) + fwd_slope(*taps)):
            q_ref[k, 8 * r : 8 * r + 8, :] = val

    def along_b(a, carry):
        for f in range(7):
            for qc in range(3):
                value = [q_ref[qc, strided(a * 80 + 8 * s + f), :] for s in range(3)]
                if f >= 4:
                    for qb, val in enumerate(fwd_value(*value)):
                        g_ref[a, 3 * qb + qc, 8 + f] = val
                    continue
                slope = [q_ref[3 + qc, strided(a * 80 + 8 * s + f), :] for s in range(3)]
                vv = fwd_value(*value)
                dv = fwd_slope(*value)
                vd = fwd_value(*slope)
                for qb in range(3):
                    g_ref[a, 3 * qb + qc, 3 * f] = vv[qb]
                    g_ref[a, 3 * qb + qc, 3 * f + 1] = dv[qb]
                    g_ref[a, 3 * qb + qc, 3 * f + 2] = vd[qb]
        return carry

    lax.fori_loop(0, PA, along_b, 0)

    zero = jnp.zeros((8, LANES), F32)

    def clear(a, carry):
        for q in range(9):
            for k in range(12):
                acc_ref[a, q, k] = zero
        return carry

    lax.fori_loop(0, 2, clear, 0)

    def points(slab, q):
        h = h_ref[slab]
        outer = jnp.where(live > slab, h, 0.0)

        def taps(slot):
            return [g_ref[slab + s, q, slot] for s in range(3)]

        grads = [
            [fwd_slope(*taps(3 * f)), fwd_value(*taps(3 * f + 1)), fwd_value(*taps(3 * f + 2))]
            for f in range(4)
        ]
        pressure = fwd_value(*taps(9))
        adv = [fwd_value(*taps(12 + c)) for c in range(3)]
        inv = 1.0 / h
        inv2 = inv * inv
        four = 4.0 * inv2
        fixed = 4.0 / DT**2 + (36.0 * NU**2) * (inv2 * inv2)
        h2 = (h * h) * (1.0 / 12.0)
        coef_f = [[None] * 3 for _ in range(4)]
        coef_k = [[[None] * 3 for _ in range(4)] for _ in range(3)]
        for t in range(3):
            a = [adv[c][t] for c in range(3)]
            conv = [
                a[0] * grads[c][0][t] + a[1] * grads[c][1][t] + a[2] * grads[c][2][t]
                for c in range(3)
            ]
            mom = [conv[c] + grads[3][c][t] for c in range(3)]
            cont = grads[0][0][t] + grads[1][1][t] + grads[2][2][t]
            total = fixed + four * (a[0] * a[0] + a[1] * a[1] + a[2] * a[2])
            tau = lax.rsqrt(total)
            press = h * pressure[t] - h2 * (total * tau) * cont
            scaled = [tau * mom[c] for c in range(3)]
            for c in range(3):
                coef_f[c][t] = h * conv[c]
                coef_k[c][3][t] = scaled[c]
                for d in range(3):
                    val = NU * grads[c][d][t] + a[d] * scaled[c]
                    coef_k[d][c][t] = val - press if d == c else val
            coef_f[3][t] = h * cont
        for c in range(4):
            parts = (
                both(coef_f[c], coef_k[0][c]),
                back_value(*coef_k[1][c]),
                back_value(*coef_k[2][c]),
            )
            for k, part in enumerate(parts):
                for s in range(2):
                    acc_ref[slab + s, q, 3 * c + k] += outer * part[s]
                acc_ref[slab + 2, q, 3 * c + k] = outer * part[2]

    def slab_loop(slab, carry):
        def point_loop(i, inner):
            for k in range(3):
                points(slab, 3 * i + k)
            return inner

        return lax.fori_loop(0, 3, point_loop, carry)

    lax.fori_loop(0, SLABS, slab_loop, 0)

    for a in range(PA):
        for k in range(6):
            q_ref[k, a * 80 + 64 : a * 80 + 72, :] = zero
            q_ref[k, a * 80 + 72 : a * 80 + 80, :] = zero

    def back_b(a, carry):
        for c in range(4):
            for qc in range(3):
                pieces = [
                    [acc_ref[a, 3 * qb + qc, 3 * c + k] for qb in range(3)] for k in range(3)
                ]
                straight = both(pieces[0], pieces[1])
                sloped = back_value(*pieces[2])
                at = strided(a * 80 + 4 + c)
                q_ref[qc, at, :] = straight[0]
                q_ref[3 + qc, at, :] = sloped[0]
                for s in range(1, 3):
                    at = strided(a * 80 + 8 * s + 4 + c)
                    q_ref[qc, at, :] += straight[s]
                    q_ref[3 + qc, at, :] += sloped[s]
        return carry

    lax.fori_loop(0, PA, back_b, 0)

    lane = lane_iota()
    pending = zero
    for r in range(ROWS):
        y = [q_ref[k, 8 * r : 8 * r + 8, :] for k in range(6)]
        column, following = pending, zero
        for k, val in enumerate(both(y[:3], y[3:])):
            off = 2 * r + k
            if off:
                val = pltpu.roll(val, off, 1)
            column = column + jnp.where(lane >= off, val, 0.0)
            following = following + jnp.where(lane < off, val, 0.0)
        out_ref[:, r * LANES : (r + 1) * LANES] = column
        pending = following
    out_ref[:, ROWS * LANES : (ROWS + 1) * LANES] = pending
    out_ref[:, COLS * LANES :] = zero


def rim_cut(col):
    return lane_iota() < min(LANES, SHARED - col * LANES)


def widen(rim_ref, wide_ref, low):
    wide_ref[...] = jnp.zeros_like(wide_ref)
    wide_ref[low : low + 4, :RIM] = rim_ref[...]


def cut_rims(x_ref, low, rim_ref):
    rim_ref[0] = x_ref[low : low + 4, :RIM]
    rim_ref[1] = x_ref[low : low + 4, LAST_COL * LANES : LAST_COL * LANES + RIM]


def main_kernel(
    live_ref, state_hbm, mesh_hbm, disp_hbm, size_hbm, rows_hbm, pen_hbm,
    base_ref,
    state_ref, mesh_ref, disp_ref, size_ref, rows_ref, pen_ref, x_ref, f_ref, q_ref, g_ref, acc_ref, h_ref, tab_ref, wide_ref,
    own_ref, part_ref, own2_ref, part2_ref, rim_ref, rim_in_ref, rim2_ref, rim2_in_ref,
    hot_ref, hi_ref, d_ref, term_ref, load_sem, send_sem, recv_sem,
):
    groups = lax.axis_size("group")
    doms = lax.axis_size("dom")
    group = lax.axis_index("group")
    dom = lax.axis_index("dom")
    stride = groups // 2
    offsets = (1, -1, stride, -stride)
    slots = [
        (group + step, dom, (group + step >= 0) & (group + step < groups)) for step in offsets
    ]
    sides = [(group, dom - 1, dom > 0), (group, dom + 1, dom < doms - 1)]
    loads = []
    for src, dst, count in ((state_hbm, state_ref, 4), (mesh_hbm, mesh_ref, 3), (disp_hbm, disp_ref, 3)):
        for c in range(count):
            loads.append(
                pltpu.make_async_copy(src.at[c], dst.at[c], load_sem.at[len(loads)])
            )
    small = (
        (size_hbm, size_ref),
        (rows_hbm.at[0, 0], rows_ref),
        (pen_hbm.at[0, 0], pen_ref),
    )
    for src, dst in small:
        loads.append(pltpu.make_async_copy(src, dst, load_sem.at[len(loads)]))
    for load in loads:
        load.start()

    barrier = pltpu.get_barrier_semaphore()
    peers = 0
    for to_group, to_dom, present in slots + sides:
        peers = peers + present.astype(jnp.int32)

        @pl.when(present)
        def _():
            pl.semaphore_signal(
                barrier, inc=1, device_id=(to_group, to_dom), device_id_type=pl.DeviceIdType.MESH
            )

    def remote(src, dst, at, to, arrive):
        return pltpu.make_async_remote_copy(
            src_ref=src,
            dst_ref=dst,
            send_sem=send_sem.at[at],
            recv_sem=recv_sem.at[arrive],
            device_id=(to[0], to[1]),
            device_id_type=pl.DeviceIdType.MESH,
        )

    def exchange(out_ref, in_ref, peers_of, sem):
        return [
            (to[2], remote(out_ref.at[k], in_ref.at[k ^ 1], sem + k, to, sem + (k ^ 1)),
             remote(out_ref.at[k], in_ref.at[k], sem + k, to, sem + k))
            for k, to in enumerate(peers_of)
        ]

    def launch(copies):
        for present, out, _ in copies:

            @pl.when(present)
            def _():
                out.start()

    def land(copies):
        for present, _, back in copies:

            @pl.when(present)
            def _():
                back.wait_recv()

    def drain(copies):
        for present, out, _ in copies:

            @pl.when(present)
            def _():
                out.wait_send()

    traces = exchange(own_ref, part_ref, slots, 0)
    traces2 = exchange(own2_ref, part2_ref, slots, 4)
    rims = exchange(rim_ref, rim_in_ref, sides, 8)
    rims2 = exchange(rim2_ref, rim2_in_ref, sides, 10)

    for load in loads[:7] + loads[10:11]:
        load.wait()
    for c in range(3):
        f_ref[4 + c : 5 + c, :CP] = state_ref[c] - mesh_ref[c]
    f_ref[7:8, :CP] = jnp.zeros((1, CP), F32)
    for c in range(4):
        f_ref[c : c + 1, :CP] = state_ref[c]
    f_ref[:, COLS * LANES :] = jnp.zeros((8, LANES), F32)
    for k in range(32):
        h_ref[k // 8, k % 8 : k % 8 + 1, :] = size_ref[:, k * LANES : (k + 1) * LANES]
    live = jnp.zeros((8, LANES), jnp.int32) + live_ref[0, 0]
    element_stage(live, f_ref, q_ref, g_ref, acc_ref, h_ref, base_ref)
    cut_rims(base_ref, 4, rim2_ref)
    pl.semaphore_wait(barrier, peers)
    launch(rims2)

    for load in loads[7:10] + loads[11:]:
        load.wait()
    for c in range(3):
        x_ref[c : c + 1, :CP] = disp_ref[c] + 0.5 * mesh_ref[c]
    x_ref[3:4, :CP] = jnp.zeros((1, CP), F32)
    for c in range(4):
        x_ref[4 + c : 5 + c, :CP] = state_ref[c]
    x_ref[:, COLS * LANES :] = jnp.zeros((8, LANES), F32)
    cut_rims(x_ref, 0, rim_ref)
    launch(rims)
    table = face_tables(x_ref, tab_ref)
    for k in range(4):
        hi, lo = locate(rows_ref[k : k + 1, :])
        hi_ref[k : k + 1, :] = hi
        hot = one_hot(lo)
        hot_ref[k] = hot
        own_ref[k] = gather_slots(table, hi, hot)
    launch(traces)

    for k, (_, _, present) in enumerate(slots):

        @pl.when(jnp.logical_not(present))
        def _():
            part_ref[k] = jnp.zeros((8, SLOTS), F32)
            part2_ref[k] = jnp.zeros((4, SLOTS), F32)

    for k, (_, _, present) in enumerate(sides):

        @pl.when(jnp.logical_not(present))
        def _():
            rim_in_ref[k] = jnp.zeros((4, RIM), F32)
            rim2_in_ref[k] = jnp.zeros((4, RIM), F32)

    land(rims2)
    widen(rim2_in_ref.at[0], wide_ref, 4)
    for col in range(21):
        val = jnp.where(rim_cut(col), take_row(wide_ref, LAST_OFF + col * LANES), 0.0)
        base_ref[:, col * LANES : (col + 1) * LANES] += val
    widen(rim2_in_ref.at[1], wide_ref, 4)
    for col in range(21):
        val = jnp.where(rim_cut(col), wide_ref[:, col * LANES : (col + 1) * LANES], 0.0)
        add_row(base_ref, LAST_COL * LANES + LAST_OFF + col * LANES, val)
    table = pair_tables(base_ref)
    for k in range(4):
        own2_ref[k] = gather_pairs(table, hi_ref[k : k + 1, :], hot_ref[k])
    launch(traces2)

    d_ref[...] = jnp.zeros_like(d_ref)
    top = lax.broadcasted_iota(jnp.int32, (8, LANES), 0) < 3
    for col in range(COLS):
        cut = slice(col * LANES, (col + 1) * LANES)
        base_ref[:, cut] = jnp.where(top, x_ref[:, cut], base_ref[:, cut])
    land(rims)
    has_prev = 0.5 * sides[0][2].astype(F32)
    has_next = 0.5 * sides[1][2].astype(F32)
    widen(rim_in_ref.at[0], wide_ref, 0)
    for col in range(21):
        cut = slice(col * LANES, (col + 1) * LANES)
        val = take_row(wide_ref, LAST_OFF + col * LANES) - x_ref[:, cut]
        base_ref[:, cut] += jnp.where(rim_cut(col) & top, has_prev * val, 0.0)
    widen(rim_in_ref.at[1], wide_ref, 0)
    for col in range(21):
        start = LAST_COL * LANES + LAST_OFF + col * LANES
        val = wide_ref[:, col * LANES : (col + 1) * LANES] - take_row(x_ref, start)
        add_row(base_ref, start, jnp.where(rim_cut(col) & top, has_next * val, 0.0))
    land(traces)
    acc = jnp.zeros((2 * 8 * TABS, LANES), F32)
    for k, (_, _, present) in enumerate(slots):
        live_slot = present.astype(F32)
        gap = (part_ref[k] - own_ref[k]) * live_slot
        term_ref[...] = gap
        term_ref[3:4, :] = jnp.zeros((1, SLOTS), F32) + live_slot
        term_ref[4:8, :] = -pen_ref[k : k + 1, :] * gap[4:8] - (0.5 * live_slot) * own2_ref[k]
        acc = acc + scatter_dot(term_ref[...], hi_ref[k : k + 1, :], 1, TABS, hot_ref[k])
    sums = acc[: 8 * TABS] + acc[8 * TABS :]
    for a in range(PA):
        add_row(d_ref, a * PLANE, sums[16 * a : 16 * a + 8])
        add_row(d_ref, a * PLANE + 9 * PC, sums[16 * a + 8 : 16 * a + 16])
    add_extra(d_ref, sums[96:104])
    for col in range(COLS):
        cut = slice(col * LANES, (col + 1) * LANES)
        d = d_ref[:, cut]
        averaged = d / (2.0 * jnp.maximum(d[3:4], 1.0))
        base_ref[:, cut] += jnp.where(top, averaged, d)

    land(traces2)
    acc = jnp.zeros((128, LANES), F32)
    for k, (_, _, present) in enumerate(slots):
        half = (0.5 * present.astype(F32)) * part2_ref[k]
        term_ref[0:4, :] = half
        term_ref[4:8, :] = half
        acc = acc + scatter_dot(term_ref[...], paired(hi_ref[k : k + 1, :]), 2, 8, hot_ref[k])
    sums = acc[:64] + acc[64:]
    low = low_half()
    for a in range(PA):
        tile = sums[8 * a : 8 * a + 8]
        add_row(base_ref, a * PLANE, jnp.where(low, 0.0, pltpu.roll(tile, 4, 0)))
        add_row(base_ref, a * PLANE + 9 * PC, jnp.where(low, 0.0, tile))
    add_extra(base_ref, jnp.where(low, 0.0, pltpu.roll(sums[48:56], 4, 0)))
    for copies in (rims, traces, rims2, traces2):
        drain(copies)


def finish_kernel(base_ref, res_ref, new_ref):
    for c in range(3):
        new_ref[c] = base_ref[c : c + 1, :CP]
    for c in range(4):
        res_ref[c] = base_ref[4 + c : 5 + c, :CP]


VMEM = pl.BlockSpec(memory_space=pltpu.VMEM)
SMEM = pl.BlockSpec(memory_space=pltpu.SMEM)
HBM = pl.BlockSpec(memory_space=pltpu.HBM)


def shaped(*shape):
    return jax.ShapeDtypeStruct(shape, F32)


def shards(state, mesh_vel, disp, elem_size, live_slabs, trace_rows, penalty):
    base = pl.pallas_call(
        main_kernel,
        out_shape=shaped(8, WIDE),
        in_specs=[SMEM] + [HBM] * 6,
        out_specs=VMEM,
        scratch_shapes=[
            pltpu.VMEM((4, 1, CP), F32),
            pltpu.VMEM((3, 1, CP), F32),
            pltpu.VMEM((3, 1, CP), F32),
            pltpu.VMEM((1, SLABS * SLOTS), F32),
            pltpu.VMEM((4, SLOTS), jnp.int32),
            pltpu.VMEM((4, SLOTS), F32),
            pltpu.VMEM((8, WIDE), F32),
            pltpu.VMEM((8, WIDE), F32),
            pltpu.VMEM((6, 8 * ROWS, LANES), F32),
            pltpu.VMEM((PA, 9, 15, 8, LANES), F32),
            pltpu.VMEM((PA, 9, 12, 8, LANES), F32),
            pltpu.VMEM((SLABS, 8, LANES), F32),
            pltpu.VMEM((8 * TABS, LANES), F32),
            pltpu.VMEM((8, RIM + LANES), F32),
            pltpu.VMEM((4, 8, SLOTS), F32),
            pltpu.VMEM((4, 8, SLOTS), F32),
            pltpu.VMEM((4, 4, SLOTS), F32),
            pltpu.VMEM((4, 4, SLOTS), F32),
            pltpu.VMEM((2, 4, RIM), F32),
            pltpu.VMEM((2, 4, RIM), F32),
            pltpu.VMEM((2, 4, RIM), F32),
            pltpu.VMEM((2, 4, RIM), F32),
            pltpu.VMEM((4, LANES, SLOTS), BF16),
            pltpu.VMEM((4, SLOTS), jnp.int32),
            pltpu.VMEM((8, WIDE), F32),
            pltpu.VMEM((8, SLOTS), F32),
            pltpu.SemaphoreType.DMA((13,)),
            pltpu.SemaphoreType.DMA((12,)),
            pltpu.SemaphoreType.DMA((12,)),
        ],
        compiler_params=pltpu.CompilerParams(
            vmem_limit_bytes=48 << 20, collective_id=0, has_side_effects=True
        ),
    )(live_slabs, *[pltpu.with_memory_space_constraint(x, pltpu.HBM) for x in (state, mesh_vel, disp, elem_size, trace_rows, penalty)])
    return pl.pallas_call(
        finish_kernel,
        out_shape=(shaped(4, 1, CP), shaped(3, 1, CP)),
        in_specs=[VMEM],
        out_specs=(VMEM, VMEM),
        compiler_params=pltpu.CompilerParams(vmem_limit_bytes=16 << 20),
    )(base)


def solution(mesh):
    return jax.shard_map(
        shards,
        mesh=mesh,
        in_specs=(
            P(None, "group", "dom"),
            P(None, "group", "dom"),
            P(None, "group", "dom"),
            P("group", "dom"),
            P("group", "dom"),
            P("group", "dom", None, None),
            P("group", "dom", None, None),
        ),
        out_specs=(P(None, "group", "dom"), P(None, "group", "dom")),
        check_vma=False,
    )
```
